256 devices in a mesh: lat: 8 (over x_hi, y), lon: 16 (over z, core), freq: 2 (over x_lo).
Axes of the slice: x: 4 (x_hi: 2, x_lo: 2; x = x_hi * 2 + x_lo), y: 4, z: 8, core: 2. Of those that a mesh axis runs over, the one named last changes fastest.
Arguments:
- spectrum: float32 [36, 36, 32, 2048], P('freq', None, 'lat', 'lon'), may hold values from 0.05 to 1
- group_speed: float32 [36], P('freq'), may hold values from 0.15 to 0.6
- sea_mask: int32 [32, 2048], P('lat', 'lon'), may hold values 0 or 1
- wind_growth: float32 [32, 2048], P('lat', 'lon'), may hold values from 0.2 to 2
- dissipation: float32 [32, 2048], P('lat', 'lon'), may hold values from 0.1 to 1
- wind_profile: float32 [1296], replicated, may hold values from 0.02 to 0.2
- nonlinear_coef: float32 [1296], replicated, may hold values from 0.05 to 0.5
- momentum: float32 [2, 1296], replicated, may hold values from -6 to 6
- quadruplet: int32 [2, 1296], replicated, may hold values from 0 to 1295, as said below
- ocean_cell: int32 [32, 2048], P('lat', 'lon'), may hold values from 0 to 65535, as said below
Outputs:
- spectrum_out: float32 [36, 36, 32, 2048], P('freq', None, 'lat', 'lon')
- ocean_stress: float32 [65536, 2], P(('lon', 'freq'))
The draws below stay inside these ranges and needn't reach their ends.
Inputs may be any that keep to these rules, and one draw needn't show every extreme that they name: quadruplet[0, b] names a bin 1 or 2 frequencies higher (at most the highest) and 1 to 6 directions further, cyclically; quadruplet[1, b] one 1 or 2 frequencies lower (at least the lowest) and 1 to 6 directions back. ocean_cell[i, j] = j * 32 + i2 with i2 within 1 of i.
All inputs are finite; a program needn't handle non-finite values. No bound on the sum of `sea_mask` on one device may be relied on, other than what follows from the above.
Results may differ from the reference program's by a relative error of at most 0.000094.
Values sent between devices are 32-bit elements; how exact they have to be, the bound alone decides.
No kernel may reach another device: no remote copies, remote signals or barrier semaphores. Data moves between devices by JAX's collectives and lax.ppermute only.
A program may use at most 64 MiB of HBM per device.

```python
import math
import jax
import jax.numpy as jnp
from jax import lax

NF = 36
NDIR = 36
NB = 1296
NLAT = 32
NLON = 2048
OCELLS = 65536


def draw_quadruplet(key, part):
    keys = jax.random.split(jax.random.fold_in(key, 7), 4)
    bins = jnp.arange(NF * NDIR)
    freqs = bins // NDIR
    directions = bins % NDIR
    up_freq = jax.random.randint(keys[0], (NF * NDIR,), 1, 3)
    up_dir = jax.random.randint(keys[1], (NF * NDIR,), 1, 7)
    down_freq = jax.random.randint(keys[2], (NF * NDIR,), 1, 3)
    down_dir = jax.random.randint(keys[3], (NF * NDIR,), 1, 7)
    higher = jnp.minimum(freqs + up_freq, NF - 1) * NDIR + (directions + up_dir) % NDIR
    lower = jnp.maximum(freqs - down_freq, 0) * NDIR + (directions - down_dir + NDIR) % NDIR
    return jnp.stack([higher, lower]).astype(jnp.int32)


def draw_ocean_cell(key, part):
    jitter = jax.random.randint(jax.random.fold_in(key, 11), (NLAT, NLON), -1, 2)
    lat_rows = jnp.arange(NLAT)[:, None]
    lon_cols = jnp.arange(NLON)[None, :]
    shifted = jnp.clip(lat_rows + jitter, 0, NLAT - 1)
    return (lon_cols * NLAT + shifted).astype(jnp.int32)


def place_ends(values, key, low, top_value):
    spot = [jax.random.randint(jax.random.fold_in(key, axis), (), 0, length) for axis, length in enumerate(values.shape)]
    main_axis = values.shape.index(max(values.shape))
    next_to = spot[:main_axis] + [(spot[main_axis] + 1) % values.shape[main_axis]] + spot[main_axis + 1:]
    return values.at[tuple(spot)].set(low).at[tuple(next_to)].set(top_value)


def steps_of(rng, extent, pieces, least, top_value):
    level, own = 1.0, jax.random.fold_in(rng, 6)
    for axis_at, shards_of in pieces:
        heights = jnp.exp(jax.random.uniform(jax.random.fold_in(own, axis_at), (shards_of,), jnp.float32, least / len(pieces), top_value / len(pieces)))
        level = level * jnp.repeat(heights, extent[axis_at] // shards_of).reshape([-1 if axis == axis_at else 1 for axis in range(len(extent))])
    return level


def noise(key, shape, deviation, reach, dtype=jnp.bfloat16):
    values = deviation * jax.random.normal(key, shape, jnp.float32)
    return jnp.clip(values, min=-reach, max=reach).astype(dtype)


def setup_inputs(seed: int = 0) -> dict:
    splits = jax.random.split(jax.random.key(seed), 11)
    spectrum = jnp.clip(0.05 + 0.95 * jax.random.uniform(splits[0], (NF, NDIR, NLAT, NLON), jnp.float32) ** steps_of(splits[0], (NF, NDIR, NLAT, NLON), ((0, 2), (2, 8), (3, 16)), -0.2, 0.2), 0.05, 1.0)
    group_speed = jnp.clip(jnp.exp(math.log(0.6) - 1.3862944 * jax.random.uniform(splits[1], (NF,), jnp.float32) ** steps_of(splits[1], (NF,), ((0, 2),), -0.2, 0.2)), 0.15, 0.6)
    sea_mask = place_ends((jax.random.randint(splits[2], (NLAT, NLON), 0, 4) < 3).astype(jnp.int32), jax.random.fold_in(splits[2], 1), 0, 1)
    wind_growth = jnp.clip(jnp.exp(math.log(2.0) - 2.3025851 * jax.random.uniform(splits[3], (NLAT, NLON), jnp.float32) ** steps_of(splits[3], (NLAT, NLON), ((0, 8), (1, 16)), -0.2, 0.2)), 0.2, 2.0)
    dissipation = jnp.clip(jnp.exp(math.log(1.0) - 2.3025851 * jax.random.uniform(splits[4], (NLAT, NLON), jnp.float32) ** steps_of(splits[4], (NLAT, NLON), ((0, 8), (1, 16)), -0.2, 0.2)), 0.1, 1.0)
    wind_profile = jnp.clip(jnp.exp(jax.random.uniform(splits[5], (NB,), jnp.float32, math.log(0.02), math.log(0.2))), 0.02, 0.2)
    nonlinear_coef = jnp.clip(jnp.exp(jax.random.uniform(splits[6], (NB,), jnp.float32, math.log(0.05), math.log(0.5))), 0.05, 0.5)
    momentum = noise(splits[7], (2, NB), 1.0, 6.0, jnp.float32)
    quadruplet = draw_quadruplet(jax.random.fold_in(splits[10], 71), 0)
    ocean_cell = draw_ocean_cell(jax.random.fold_in(splits[10], 71), 0)
    return {"spectrum": spectrum, "group_speed": group_speed, "sea_mask": sea_mask, "wind_growth": wind_growth, "dissipation": dissipation, "wind_profile": wind_profile, "nonlinear_coef": nonlinear_coef, "momentum": momentum, "quadruplet": quadruplet, "ocean_cell": ocean_cell}


time_step = 0.5


def propagate_all(spectrum, group_speed, sea_mask):
    ndirs = spectrum.shape[1]
    angles = 2.0 * jnp.pi * jnp.arange(ndirs).astype(jnp.float32) / ndirs
    speed_x = (group_speed[:, None] * jnp.cos(angles)[None, :])[:, :, None, None]
    speed_y = (group_speed[:, None] * jnp.sin(angles)[None, :])[:, :, None, None]
    west = jnp.roll(spectrum, 1, axis=3)
    east = jnp.roll(spectrum, -1, axis=3)
    padded = jnp.pad(spectrum, ((0, 0), (0, 0), (1, 1), (0, 0)))
    south = padded[:, :, :-2, :]
    north = padded[:, :, 2:, :]
    moved = (spectrum - jnp.maximum(speed_x, 0.0) * (spectrum - west) - jnp.minimum(speed_x, 0.0) * (east - spectrum)
             - jnp.maximum(speed_y, 0.0) * (spectrum - south) - jnp.minimum(speed_y, 0.0) * (north - spectrum))
    return moved * sea_mask.astype(jnp.float32)[None, None]


def reference(spectrum, group_speed, sea_mask, wind_growth, dissipation, wind_profile, nonlinear_coef, momentum, quadruplet, ocean_cell):
    highest = lax.Precision.HIGHEST
    moved = propagate_all(spectrum, group_speed, sea_mask)
    nbins = NF * NDIR
    flat_moved = moved.reshape(nbins, -1)
    weights = momentum * wind_profile[None, :]
    stress = jnp.dot(weights, flat_moved, precision=highest) * wind_growth.reshape(-1)[None, :]
    ocean_stress = jax.ops.segment_sum(stress.T, ocean_cell.reshape(-1), OCELLS)

    def one_row(packed):
        energy_row, wind_row, dissip_row, mask_row = packed
        flat_bins = energy_row.reshape(nbins, -1)
        third = flat_bins[quadruplet[0]]
        fourth = flat_bins[quadruplet[1]]
        transfer = nonlinear_coef[:, None] * (flat_bins * flat_bins * (third + fourth) - 2.0 * flat_bins * third * fourth)
        scattered = jnp.zeros_like(transfer).at[quadruplet[0]].add(transfer).at[quadruplet[1]].add(transfer)
        energy = jnp.mean(flat_bins, axis=0)
        tendency = (wind_row[None, :] * wind_profile[:, None] * flat_bins + scattered - 2.0 * transfer
                    - dissip_row[None, :] * energy[None, :] * flat_bins)
        result = mask_row[None, :] * (flat_bins + time_step * tendency)
        return result.reshape(energy_row.shape)

    by_rows = jnp.moveaxis(moved, 2, 0)
    updated = lax.map(one_row, (by_rows, wind_growth, dissipation, sea_mask.astype(jnp.float32)))
    spectrum_out = jnp.moveaxis(updated, 0, 2)
    return spectrum_out, ocean_stress
```

```python
import jax
import jax.numpy as jnp
import numpy as np
from jax import lax
from jax.experimental import pallas as pl
from jax.experimental.pallas import tpu as pltpu
from jax.sharding import PartitionSpec as P

F32 = jnp.float32
NF, ND = 18, 36
NB = NF * ND
TILES = ND // 2
ROWS = NB * 4
BORDER = 4 * ND

angles = (np.float32(2.0 * np.pi) * np.arange(ND, dtype=np.float32) / np.float32(ND)).astype(np.float32)
COS = np.cos(angles).astype(np.float32)
SIN = np.sin(angles).astype(np.float32)
WEST = [bool(c > 0) for c in COS]
WEST_TILES = [k for k in range(TILES) if WEST[2 * k] or WEST[2 * k + 1]]
EAST_TILES = [k for k in range(TILES) if not (WEST[2 * k] and WEST[2 * k + 1])]
LANES_F = 10
FREQS_V = 12

VM = pl.BlockSpec(memory_space=pltpu.VMEM)
SM = pl.BlockSpec(memory_space=pltpu.SMEM)
PARAMS = pltpu.CompilerParams(vmem_limit_bytes=40 * 1024 * 1024)


def in_vmem(shape, dtype=F32):
    return pltpu.VMEM(shape, dtype)


def tile_iota(dim):
    return lax.broadcasted_iota(jnp.int32, (8, 128), dim)


def pack_kernel(e_ref, up_ref, dn_ref, east_ref, west_ref):
    lane = tile_iota(1)
    for f in range(NF):
        up_ref[f * 18 : f * 18 + 18, :] = e_ref[pl.ds(f * 144 + 3, 18, stride=4), :]
        dn_ref[f * 18 : f * 18 + 18, :] = e_ref[pl.ds(f * 144 + 72, 18, stride=4), :]
    for tiles, ref, col in ((WEST_TILES, east_ref, 127), (EAST_TILES, west_ref, 0)):
        for chunk in range(2):
            acc = jnp.zeros((8, 128), F32)
            for f in range(chunk * FREQS_V, min(NF, (chunk + 1) * FREQS_V)):
                for kk, k in enumerate(tiles):
                    pos = (f % FREQS_V) * LANES_F + kk
                    x = e_ref[(f * TILES + k) * 8 : (f * TILES + k) * 8 + 8, :]
                    acc = jnp.where(lane == pos, pltpu.roll(x, (pos - col) % 128, 1), acc)
            ref[:, chunk * 128 : chunk * 128 + 128] = acc


def move_kernel(
    where_ref, gs_ref, mom_ref, prof_ref, e_ref, so_ref, no_ref, hw_ref, he_ref, mask_ref, wind_ref, cell_ref,
    moved_ref, msg_ref, halo_ref,
):
    lat, lon, freq = where_ref[0], where_ref[1], where_ref[2]
    lane, row = tile_iota(1), tile_iota(0)
    first, last = lane == 0, lane == 127
    low = row < 4
    top, bottom = row % 4 == 0, row % 4 == 3
    for f in range(NF):
        halo_ref[pl.ds(f * 144, 18, stride=4), :] = so_ref[f * 18 : f * 18 + 18, :]
        halo_ref[pl.ds(f * 144 + 72 + 3, 18, stride=4), :] = no_ref[f * 18 : f * 18 + 18, :]
    mask4 = mask_ref[...].astype(F32)
    mask8 = jnp.concatenate([mask4, mask4], 0)

    def one_freq(f, carry):
        en, t0, t1 = carry
        chunk = pl.multiple_of((f // FREQS_V) * 128, 128)
        base = (f % FREQS_V) * LANES_F
        back = lax.rem(128 - base, 128)
        hw = pltpu.roll(hw_ref[:, pl.ds(chunk, 128)], back, 1)
        he = pltpu.roll(he_ref[:, pl.ds(chunk, 128)], back, 1)
        gs = gs_ref[f]
        for k in range(TILES):
            at = pl.multiple_of(f * 144 + k * 8, 8)
            x = e_ref[pl.ds(at, 8), :]
            h = halo_ref[pl.ds(at, 8), :]
            west = east = None
            if k in WEST_TILES:
                kk = WEST_TILES.index(k)
                west = jnp.where(first, pltpu.roll(hw, (128 - kk) % 128, 1), pltpu.roll(x, 1, 1))
            if k in EAST_TILES:
                kk = EAST_TILES.index(k)
                east = jnp.where(last, pltpu.roll(he, 127 - kk, 1), pltpu.roll(x, 127, 1))
            if east is None:
                xs = west
            elif west is None:
                xs = east
            else:
                xs = jnp.where(low, west, east) if WEST[2 * k] else jnp.where(low, east, west)
            if k < TILES // 2:
                ys = jnp.where(top, h, pltpu.roll(x, 1, 0))
            else:
                ys = jnp.where(bottom, h, pltpu.roll(x, 7, 0))
            cx = jnp.where(low, float(abs(COS[2 * k])), float(abs(COS[2 * k + 1]))).astype(F32)
            cy = jnp.where(low, float(abs(SIN[2 * k])), float(abs(SIN[2 * k + 1]))).astype(F32)
            m = mask8 * (x - gs * (cx * (x - xs) + cy * (x - ys)))
            moved_ref[pl.ds(at, 8), :] = m
            b = freq * NB + f * ND + 2 * k
            p0, p1 = prof_ref[b], prof_ref[b + 1]
            en = en + m
            t0 = t0 + m * jnp.where(low, mom_ref[0, b] * p0, mom_ref[0, b + 1] * p1)
            t1 = t1 + m * jnp.where(low, mom_ref[1, b] * p0, mom_ref[1, b + 1] * p1)
        return en, t0, t1

    zero = jnp.zeros((8, 128), F32)
    en, t0, t1 = lax.fori_loop(0, NF, one_freq, (zero, zero, zero))
    start = pl.multiple_of((1 - freq) * (14 * 144), 8)
    for k in range(72):
        msg_ref[k * 8 : k * 8 + 8, :] = moved_ref[pl.ds(start + k * 8, 8), :]
    wind = wind_ref[...]
    i4 = lax.broadcasted_iota(jnp.int32, (4, 128), 0) + lat * 4
    j4 = lax.broadcasted_iota(jnp.int32, (4, 128), 1) + lon * 128
    offset = cell_ref[...] - (j4 * 32 + i4)
    for c, t in enumerate((t0, t1)):
        tau = (t[0:4] + t[4:8]) * wind
        at = 4 * BORDER + 8 * c
        msg_ref[at : at + 8, :] = zero
        for d in (-1, 0, 1):
            msg_ref[at + 1 + d : at + 5 + d, :] += jnp.where(offset == d, tau, 0.0)
    msg_ref[4 * BORDER + 16 : 4 * BORDER + 20, :] = en[0:4] + en[4:8]
    msg_ref[4 * BORDER + 20 : 4 * BORDER + 24, :] = jnp.zeros((4, 128), F32)


def transfer_of(e, third, fourth, coef):
    return coef * (e * (e * (third + fourth) - 2.0 * third * fourth))


STEP = 8


def inner_kernel(where_ref, quad_ref, coef_ref, m_ref, a_ref, b_ref):
    freq = where_ref[2]
    zero = jnp.zeros((4, 128), F32)

    def clear(i, _):
        for u in range(8):
            a_ref[i * 8 + u] = zero
            b_ref[i * 8 + u] = zero
        return 0

    lax.fori_loop(0, NB // 8, clear, 0)
    shift = freq * NB
    start = freq * (2 * ND)

    def some(i, _):
        own, q0, q1, t = [], [], [], []
        for u in range(STEP):
            b = start + i * STEP + u
            own.append(b)
            q0.append(quad_ref[0, shift + b] - shift)
            q1.append(quad_ref[1, shift + b] - shift)
            t.append(transfer_of(m_ref[b], m_ref[q0[u]], m_ref[q1[u]], coef_ref[shift + b]))
        for u in range(STEP):
            a_ref[q0[u]] += t[u]
            b_ref[q1[u]] += t[u]
        for u in range(STEP):
            a_ref[own[u]] -= 2.0 * t[u]
        return 0

    lax.fori_loop(0, 16 * ND // STEP, some, 0)


def outer_kernel(
    where_ref, quad_ref, coef_ref, prof_ref, m_ref, a_ref, b_ref, mine_ref, theirs_ref, wind_ref, dis_ref,
    out_ref, ext_ref, acc_ref,
):
    freq = where_ref[2]
    zero = jnp.zeros((4, 128), F32)
    mine = freq * BORDER
    theirs = BORDER - mine

    def fill(i, _):
        for u in range(8):
            k = i * 8 + u
            ext_ref[mine + k] = mine_ref[k]
            ext_ref[theirs + k] = theirs_ref[k]
            acc_ref[k] = zero
            acc_ref[BORDER + k] = zero
        return 0

    lax.fori_loop(0, BORDER // 8, fill, 0)
    shift = 14 * ND

    def some(i, _):
        own, q0, q1, t = [], [], [], []
        for u in range(STEP):
            b = 2 * ND + i * STEP + u
            own.append(b)
            q0.append(quad_ref[0, shift + b] - shift)
            q1.append(quad_ref[1, shift + b] - shift)
            t.append(transfer_of(ext_ref[b], ext_ref[q0[u]], ext_ref[q1[u]], coef_ref[shift + b]))
        for u in range(STEP):
            acc_ref[q0[u]] += t[u]
            acc_ref[q1[u]] += t[u]
            acc_ref[own[u]] -= 2.0 * t[u]
        return 0

    lax.fori_loop(0, BORDER // STEP, some, 0)
    energy = (mine_ref[BORDER + 4] + theirs_ref[BORDER + 4]) * (1.0 / (2 * NB))
    keep = 1.0 - 0.5 * (dis_ref[...] * energy)
    wind = 0.5 * wind_ref[...]
    first = freq * NB

    def finish(b, extra):
        out = m_ref[b] * (keep + wind * prof_ref[first + b])
        total = a_ref[b] + b_ref[b]
        if extra is not None:
            total = total + extra
        out_ref[b] = out + 0.5 * total

    inner = freq * BORDER
    edge = (1 - freq) * (14 * ND)

    def plain(i, _):
        for u in range(8):
            finish(inner + i * 8 + u, None)
        return 0

    lax.fori_loop(0, 14 * ND // 8, plain, 0)

    def bordering(i, _):
        for u in range(8):
            k = i * 8 + u
            finish(edge + k, acc_ref[mine + k])
        return 0

    lax.fori_loop(0, BORDER // 8, bordering, 0)


def half_kernel(where_ref, mine_ref, theirs_ref, out_ref):
    freq = where_ref[2]
    lane = tile_iota(1)
    at = 4 * BORDER
    r0 = mine_ref[at : at + 8, :] + theirs_ref[at : at + 8, :]
    r1 = mine_ref[at + 8 : at + 16, :] + theirs_ref[at + 8 : at + 16, :]
    lower = jnp.where(lane < 64, r0, pltpu.roll(r1, 64, 1))
    upper = jnp.where(lane < 64, pltpu.roll(r0, 64, 1), r1)
    out_ref[...] = jnp.where(freq == 0, lower, upper)


def cells_kernel(where_ref, r_ref, out_ref, z_ref, t_ref):
    lat = where_ref[0]
    z_ref[...] = jnp.zeros_like(z_ref)
    for k in range(8):
        block = r_ref[pl.ds(pl.multiple_of(jnp.bitwise_xor(lat, k) * 8, 8), 8), :]
        z_ref[7 + 4 * k : 13 + 4 * k, :] += block[0:6]
    t_ref[:, 0:32] = jnp.transpose(z_ref[8:40, :])
    t_ref[:, 32:128] = jnp.zeros((128, 96), F32)
    out = jnp.zeros((32, 128), F32)
    for jj in range(4):
        piece = t_ref[pl.ds(jj, 32, stride=4), :]
        out = out + pltpu.roll(piece, jj * 32, 1)
    for c in range(2):
        for g in range(16):
            out_ref[c : c + 1, g * 128 : g * 128 + 128] = out[c * 16 + g : c * 16 + g + 1, :]


def call(kernel, out, in_specs, scratch=()):
    return pl.pallas_call(
        kernel,
        out_shape=out,
        in_specs=in_specs,
        out_specs=jax.tree.map(lambda _: VM, out),
        scratch_shapes=list(scratch),
        compiler_params=PARAMS,
    )


def local(
    spectrum, group_speed, sea_mask, wind_growth, dissipation, wind_profile, nonlinear_coef, momentum, quadruplet,
    ocean_cell,
):
    where = jnp.stack([lax.axis_index(a) for a in ("lat", "lon", "freq")]).astype(jnp.int32)
    flat = spectrum.reshape(ROWS, 128)
    halo = in_vmem((NF * 18, 128))
    edge = in_vmem((8, 256))
    up, dn, to_east, to_west = call(pack_kernel, (halo, halo, edge, edge), [VM])(flat)
    nlat, nlon = lax.axis_size("lat"), lax.axis_size("lon")
    east = [(i, (i + 1) % nlon) for i in range(nlon)]
    north = [(i, i + 1) for i in range(nlat - 1)]
    from_west = lax.ppermute(to_east, "lon", east)
    from_east = lax.ppermute(to_west, "lon", [(j, i) for i, j in east])
    from_south = lax.ppermute(up, "lat", north)
    from_north = lax.ppermute(dn, "lat", [(j, i) for i, j in north])
    moved, message = call(
        move_kernel,
        (in_vmem((ROWS, 128)), in_vmem((4 * BORDER + 24, 128))),
        [SM] * 4 + [VM] * 8,
        [pltpu.VMEM((ROWS, 128), F32)],
    )(
        where, group_speed, momentum, wind_profile, flat, from_south, from_north, from_west, from_east, sea_mask,
        wind_growth, ocean_cell,
    )
    theirs = lax.ppermute(message, "freq", [(0, 1), (1, 0)])
    bins = moved.reshape(NB, 4, 128)
    acc = in_vmem((NB, 4, 128))
    part_a, part_b = call(inner_kernel, (acc, acc), [SM] * 3 + [VM])(where, quadruplet, nonlinear_coef, bins)
    rows = call(half_kernel, in_vmem((8, 128)), [SM, VM, VM])(where, message, theirs)
    for bit in (1, 2, 4):
        other = lax.ppermute(rows, "lat", [(i, i ^ bit) for i in range(nlat)])
        rows = jnp.concatenate([rows, other], 0)
    out = call(
        outer_kernel,
        jax.ShapeDtypeStruct((NB, 4, 128), F32),
        [SM] * 4 + [VM] * 7,
        [pltpu.VMEM((2 * BORDER, 4, 128), F32), pltpu.VMEM((2 * BORDER, 4, 128), F32)],
    )(
        where, quadruplet, nonlinear_coef, wind_profile, bins, part_a, part_b, message.reshape(BORDER + 6, 4, 128),
        theirs.reshape(BORDER + 6, 4, 128), wind_growth, dissipation,
    )
    stress = call(
        cells_kernel,
        jax.ShapeDtypeStruct((2, 2048), F32),
        [SM, VM],
        [pltpu.VMEM((48, 128), F32), pltpu.VMEM((128, 128), F32)],
    )(where, rows)
    return out.reshape(spectrum.shape), stress.T


def solution(mesh):
    return jax.shard_map(
        local,
        mesh=mesh,
        in_specs=(
            P("freq", None, "lat", "lon"),
            P("freq"),
            P("lat", "lon"),
            P("lat", "lon"),
            P("lat", "lon"),
            P(),
            P(),
            P(),
            P(),
            P("lat", "lon"),
        ),
        out_specs=(P("freq", None, "lat", "lon"), P(("lon", "freq"), None)),
        check_vma=False,
    )
```

```python
import jax
import jax.numpy as jnp
import numpy as np
from jax import lax
from jax.experimental import pallas as pl
from jax.experimental.pallas import tpu as pltpu
from jax.sharding import PartitionSpec as P

F32 = jnp.float32
NF, ND = 18, 36
NB = NF * ND
TILES = ND // 2
ROWS = NB * 4
BORDER = 4 * ND

angles = (np.float32(2.0 * np.pi) * np.arange(ND, dtype=np.float32) / np.float32(ND)).astype(np.float32)
COS = np.cos(angles).astype(np.float32)
SIN = np.sin(angles).astype(np.float32)
WEST = [bool(c > 0) for c in COS]
WEST_TILES = [k for k in range(TILES) if WEST[2 * k] or WEST[2 * k + 1]]
EAST_TILES = [k for k in range(TILES) if not (WEST[2 * k] and WEST[2 * k + 1])]
LANES_F = 10
FREQS_V = 6

VM = pl.BlockSpec(memory_space=pltpu.VMEM)
HB = pl.BlockSpec(memory_space=pltpu.HBM)
ANY = pl.BlockSpec(memory_space=pl.ANY)
SM = pl.BlockSpec(memory_space=pltpu.SMEM)
PARAMS = pltpu.CompilerParams(vmem_limit_bytes=16 * 1024 * 1024)


def in_vmem(shape, dtype=F32):
    return pltpu.VMEM(shape, dtype)


def tile_iota(dim):
    return lax.broadcasted_iota(jnp.int32, (8, 128), dim)


def twice(x):
    return jnp.concatenate([x, x], 0)


CHUNK = 6


def pack_kernel(hbm_ref, e_ref, far_ref, near_ref, across_ref, inside_ref, sems):
    lane = tile_iota(1)
    odd_lat = lax.axis_index("lat") % 2 == 1
    odd_lon = lax.axis_index("lon") % 2 == 1
    up, down = 3, 72
    far, near = jnp.where(odd_lat, up, down), jnp.where(odd_lat, down, up)
    copies = []
    for c in range(NF // CHUNK):
        part = pl.ds(c * CHUNK * 144, CHUNK * 144)
        copies.append(pltpu.make_async_copy(hbm_ref.at[part], e_ref.at[part], sems.at[c]))
        copies[c].start()
    acc = [[jnp.zeros((8, 128), F32)] * 3, [jnp.zeros((8, 128), F32)] * 3]
    for f in range(NF):
        if f % CHUNK == 0:
            copies[f // CHUNK].wait()
        far_ref[f * 18 : f * 18 + 18, :] = e_ref[pl.ds(f * 144 + far, 18, stride=4), :]
        near_ref[f * 18 : f * 18 + 18, :] = e_ref[pl.ds(f * 144 + near, 18, stride=4), :]
        chunk = f // FREQS_V
        for side, tiles, col in ((0, WEST_TILES, 127), (1, EAST_TILES, 0)):
            for kk, k in enumerate(tiles):
                pos = (f % FREQS_V) * LANES_F + kk
                x = e_ref[(f * TILES + k) * 8 : (f * TILES + k) * 8 + 8, :]
                acc[side][chunk] = jnp.where(lane == pos, pltpu.roll(x, (pos - col) % 128, 1), acc[side][chunk])
    for chunk in range(3):
        across_ref[:, chunk * 128 : chunk * 128 + 128] = jnp.where(odd_lon, acc[0][chunk], acc[1][chunk])
        inside_ref[:, chunk * 128 : chunk * 128 + 128] = jnp.where(odd_lon, acc[1][chunk], acc[0][chunk])


EXT = 22 * ND
EXT_ROWS = EXT * 4
SUMS = 6


def table_kernel(
    gs_ref, mom_ref, prof_ref, coef_ref, mask_ref, wind_ref, cx_ref, cy_ref, w0_ref, w1_ref, pw_ref, half_ref, *zeros
):
    freq = lax.axis_index("freq")
    first = freq * NB
    low = tile_iota(0) < 4
    mask8 = twice(mask_ref[...].astype(F32))
    wind8 = twice(wind_ref[...]) * 0.5
    zero = jnp.zeros((8, 128), F32)

    def one_freq(f, _):
        speed = gs_ref[f] * mask8
        for k in range(TILES):
            at = pl.ds(pl.multiple_of(f * 144 + k * 8, 8), 8)
            b = first + f * ND + 2 * k
            p0, p1 = prof_ref[b], prof_ref[b + 1]
            cx_ref[at, :] = speed * jnp.where(low, float(abs(COS[2 * k])), float(abs(COS[2 * k + 1])))
            cy_ref[at, :] = speed * jnp.where(low, float(abs(SIN[2 * k])), float(abs(SIN[2 * k + 1])))
            pt = jnp.where(low, p0, p1)
            w0_ref[at, :] = pt * jnp.where(low, mom_ref[0, b], mom_ref[0, b + 1])
            w1_ref[at, :] = pt * jnp.where(low, mom_ref[1, b], mom_ref[1, b + 1])
            pw_ref[at, :] = wind8 * pt
        return 0

    lax.fori_loop(0, NF, one_freq, 0)

    def one_ext(f, _):
        for k in range(TILES):
            at = pl.ds(pl.multiple_of(f * 144 + k * 8, 8), 8)
            b = freq * (14 * ND) + f * ND + 2 * k
            half_ref[at, :] = jnp.where(low, 0.5 * coef_ref[b], 0.5 * coef_ref[b + 1])
            for z in zeros:
                z[at, :] = zero
        return 0

    lax.fori_loop(0, EXT // ND, one_ext, 0)


def move_kernel(
    e_ref, far_ref, near_ref, across_ref, inside_ref, mask_ref, wind_ref, cell_ref, cx_ref, cy_ref, w0_ref, w1_ref,
    moved_ref, big_ref, small_ref, own_ref, halo_ref, half_ref,
):
    lat, lon, freq = lax.axis_index("lat"), lax.axis_index("lon"), lax.axis_index("freq")
    lane, row = tile_iota(1), tile_iota(0)
    first, last = lane == 0, lane == 127
    low = row < 4
    top, bottom = row % 4 == 0, row % 4 == 3
    odd_lat, odd_lon = lat % 2 == 1, lon % 2 == 1
    south, north = 0, 75
    far, near = jnp.where(odd_lat, north, south), jnp.where(odd_lat, south, north)
    for f in range(NF):
        halo_ref[pl.ds(f * 144 + far, 18, stride=4), :] = far_ref[f * 18 : f * 18 + 18, :]
        halo_ref[pl.ds(f * 144 + near, 18, stride=4), :] = near_ref[f * 18 : f * 18 + 18, :]
    mask8 = twice(mask_ref[...].astype(F32))
    own = freq * (4 * BORDER)

    def some_freqs(c, carry):
        en, t0, t1 = carry
        across = across_ref[:, pl.ds(pl.multiple_of(c * 128, 128), 128)]
        inside = inside_ref[:, pl.ds(pl.multiple_of(c * 128, 128), 128)]
        hw, he = jnp.where(odd_lon, inside, across), jnp.where(odd_lon, across, inside)
        for f in range(FREQS_V):
            for k in range(TILES):
                at = pl.multiple_of((c * FREQS_V + f) * 144 + k * 8, 8)
                x = e_ref[pl.ds(at, 8), :]
                h = halo_ref[pl.ds(at, 8), :]
                west = east = None
                if k in WEST_TILES:
                    pos = f * LANES_F + WEST_TILES.index(k)
                    west = jnp.where(first, pltpu.roll(hw, (128 - pos) % 128, 1), pltpu.roll(x, 1, 1))
                if k in EAST_TILES:
                    pos = f * LANES_F + EAST_TILES.index(k)
                    east = jnp.where(last, pltpu.roll(he, 127 - pos, 1), pltpu.roll(x, 127, 1))
                if east is None:
                    side = west
                elif west is None:
                    side = east
                else:
                    side = jnp.where(low, west, east) if WEST[2 * k] else jnp.where(low, east, west)
                if k < TILES // 2:
                    beside = jnp.where(top, h, pltpu.roll(x, 1, 0))
                else:
                    beside = jnp.where(bottom, h, pltpu.roll(x, 7, 0))
                m = mask8 * x - cx_ref[pl.ds(at, 8), :] * (x - side) - cy_ref[pl.ds(at, 8), :] * (x - beside)
                moved_ref[pl.ds(pl.multiple_of(own + at, 8), 8), :] = m
                en = en + m
                t0 = t0 + m * w0_ref[pl.ds(at, 8), :]
                t1 = t1 + m * w1_ref[pl.ds(at, 8), :]
        return en, t0, t1

    zero = jnp.zeros((8, 128), F32)
    en, t0, t1 = lax.fori_loop(0, NF // FREQS_V, some_freqs, (zero, zero, zero))
    start = pl.multiple_of(own + (1 - freq) * (14 * 144), 8)
    for k in range(72):
        big_ref[k * 8 : k * 8 + 8, :] = moved_ref[pl.ds(start + k * 8, 8), :]
    wind = wind_ref[...]
    i4 = lax.broadcasted_iota(jnp.int32, (4, 128), 0) + lat * 4
    j4 = lax.broadcasted_iota(jnp.int32, (4, 128), 1) + lon * 128
    offset = cell_ref[...] - (j4 * 32 + i4)
    for c, t in enumerate((t0, t1)):
        tau = (t[0:4] + t[4:8]) * wind
        half_ref[8 * c : 8 * c + 8, :] = zero
        for d in (-1, 0, 1):
            half_ref[8 * c + 1 + d : 8 * c + 5 + d, :] += jnp.where(offset == d, tau, 0.0)
    r0, r1 = half_ref[0:8, :], half_ref[8:16, :]
    lower = jnp.where(lane < 64, r0, pltpu.roll(r1, 64, 1))
    upper = jnp.where(lane < 64, pltpu.roll(r0, 64, 1), r1)
    own_ref[0:8, :] = jnp.where(freq == 0, lower, upper)
    small_ref[0:8, :] = jnp.where(freq == 0, upper, lower)
    total = twice(en[0:4] + en[4:8])
    own_ref[8:16, :] = total
    small_ref[8:16, :] = total


def transfers(own, quads, m_ref, half_ref):
    q0, q1 = quads
    e, third, fourth = [m_ref[b] for b in own], [m_ref[b] for b in q0], [m_ref[b] for b in q1]
    half = [half_ref[b] for b in own]
    return [
        half[i] * (e[i] * (e[i] * (third[i] + fourth[i]) - 2.0 * third[i] * fourth[i])) for i in range(len(own))
    ]


def add_all(quads, t, refs):
    q0, q1 = quads
    n = range(len(t))
    up = [refs[i % 3][q0[i]] for i in n]
    down = [refs[3 + i % 3][q1[i]] for i in n]
    for i in n:
        refs[i % 3][q0[i]] = up[i] + t[i]
    for i in n:
        refs[3 + i % 3][q1[i]] = down[i] + t[i]


def inner_kernel(up_ref, down_ref, half_ref, m_ref, *rest):
    refs, t_ref = rest[SUMS : 2 * SUMS], rest[2 * SUMS]
    freq = lax.axis_index("freq")
    start = freq * (6 * ND)
    shift = freq * (14 * ND)

    def one_dir(d, _):
        own = [start + d + f * ND for f in range(16)]
        quads = [[ref[shift + b] - shift for b in own] for ref in (up_ref, down_ref)]
        t = transfers(own, quads, m_ref, half_ref)
        add_all(quads, t, refs)
        for b, x in zip(own, t):
            t_ref[b] = x
        return 0

    lax.fori_loop(0, ND, one_dir, 0)


def keep_of(mine_ref, theirs_ref, dis_ref):
    energy = (mine_ref[8:16, :] + theirs_ref[8:16, :]) * (1.0 / (2 * NB))
    return 1.0 - 0.5 * (twice(dis_ref[...]) * energy)


def finish(at, own, keep, m_ref, pw_ref, parts, t_ref):
    here = pl.ds(pl.multiple_of(at, 8), 8)
    total = parts[0][here, :]
    for part in parts[1:]:
        total = total + part[here, :]
    grown = m_ref[here, :] * (keep + pw_ref[pl.ds(pl.multiple_of(at - own, 8), 8), :])
    return grown + (total - 2.0 * t_ref[here, :])


PLAIN = 14 * 144


def plain_kernel(m_ref, pw_ref, *rest):
    parts, (t_ref, mine_ref, theirs_ref, dis_ref, hbm_ref, out_ref, sems) = rest[:SUMS], rest[SUMS:]
    freq = lax.axis_index("freq")
    own = freq * (4 * BORDER)
    start = freq * (8 * 144)
    keep = keep_of(mine_ref, theirs_ref, dis_ref)
    copies = []
    for c in range(2):
        def some(i, _):
            for u in range(TILES):
                to = c * (PLAIN // 2) + i * 144 + u * 8
                out_ref[pl.ds(pl.multiple_of(to, 8), 8), :] = finish(start + to, own, keep, m_ref, pw_ref, parts, t_ref)
            return 0

        lax.fori_loop(0, 7, some, 0)
        copies.append(
            pltpu.make_async_copy(
                out_ref.at[pl.ds(c * (PLAIN // 2), PLAIN // 2)],
                hbm_ref.at[pl.ds(pl.multiple_of(own + c * (PLAIN // 2), 8), PLAIN // 2)],
                sems.at[c],
            )
        )
        copies[c].start()
    for copy in copies:
        copy.wait()


def extend_kernel(up_ref, down_ref, half_ref, theirs_ref, *rest):
    m_ref, *refs, t_ref = rest[SUMS + 2 :]
    freq = lax.axis_index("freq")
    to = (1 - freq) * NB
    for k in range(BORDER):
        m_ref[to + k] = theirs_ref[k]
    shift = freq * (14 * ND)
    start = 16 * ND - shift

    def some(i, _):
        for u in range(2):
            own = [start + i * 2 + u + f * ND for f in range(4)]
            quads = [[ref[shift + b] - shift for b in own] for ref in (up_ref, down_ref)]
            t = transfers(own, quads, m_ref, half_ref)
            add_all(quads, t, refs)
            for b, x in zip(own, t):
                t_ref[b] = x
        return 0

    lax.fori_loop(0, ND // 2, some, 0)


def outer_kernel(m_ref, pw_ref, *rest):
    parts, (t_ref, mine_ref, theirs_ref, dis_ref, _, hbm_ref, out_ref, sem) = rest[:SUMS], rest[SUMS:]
    freq = lax.axis_index("freq")
    own = freq * (4 * BORDER)
    start = 14 * 144 - freq * (10 * 144)
    keep = keep_of(mine_ref, theirs_ref, dis_ref)
    for u in range(72):
        out_ref[u * 8 : u * 8 + 8, :] = finish(start + u * 8, own, keep, m_ref, pw_ref, parts, t_ref)
    copy = pltpu.make_async_copy(
        out_ref, hbm_ref.at[pl.ds(pl.multiple_of((1 - freq) * (14 * 144), 8), 4 * BORDER)], sem
    )
    copy.start()
    copy.wait()


def cells_kernel(r_ref, out_ref, z_ref, t_ref):
    lat = lax.axis_index("lat")
    z_ref[...] = jnp.zeros_like(z_ref)
    for k in range(8):
        block = r_ref[pl.ds(pl.multiple_of(jnp.bitwise_xor(lat, k) * 8, 8), 8), :]
        z_ref[7 + 4 * k : 13 + 4 * k, :] += block[0:6]
    t_ref[:, 0:32] = jnp.transpose(z_ref[8:40, :])
    t_ref[:, 32:128] = jnp.zeros((128, 96), F32)
    out = jnp.zeros((32, 128), F32)
    for jj in range(4):
        piece = t_ref[pl.ds(jj, 32, stride=4), :]
        out = out + pltpu.roll(piece, jj * 32, 1)
    for c in range(2):
        for g in range(16):
            out_ref[c : c + 1, g * 128 : g * 128 + 128] = out[c * 16 + g : c * 16 + g + 1, :]


def call(kernel, out, in_specs, scratch=(), out_specs=None, us=1.0, aliases=None):
    return pl.pallas_call(
        kernel,
        out_shape=out,
        in_specs=in_specs,
        out_specs=jax.tree.map(lambda _: VM, out) if out_specs is None else out_specs,
        scratch_shapes=list(scratch),
        compiler_params=PARAMS,
        input_output_aliases=aliases or {},
        cost_estimate=pl.CostEstimate(flops=0, transcendentals=0, bytes_accessed=int(us * 3.0e6)),
    )


def local(
    spectrum, group_speed, sea_mask, wind_growth, dissipation, wind_profile, nonlinear_coef, momentum, quadruplet,
    ocean_cell,
):
    grid = in_vmem((ROWS, 128))
    halo = in_vmem((NF * 18, 128))
    edge = in_vmem((8, 384))
    flat, far, near, across, inside = call(
        pack_kernel, (grid, halo, halo, edge, edge), [HB], [pltpu.SemaphoreType.DMA((NF // CHUNK,))]
    )(pltpu.with_memory_space_constraint(spectrum.reshape(ROWS, 128), pltpu.HBM))
    nlat, nlon = lax.axis_size("lat"), lax.axis_size("lon")

    def pairs(first, count, size):
        both = [(i, (i + 1) % size) for i in range(first, first + 2 * count, 2)]
        return both + [(j, i) for i, j in both]

    swap = pairs(0, 1, 2)
    far = lax.ppermute(far, "lat", pairs(1, nlat // 2 - 1, nlat))
    near = lax.ppermute(near, "lat", pairs(0, nlat // 2, nlat))
    across = lax.ppermute(across, "lon", pairs(1, nlon // 2, nlon))
    inside = lax.ppermute(inside, "lon", pairs(0, nlon // 2, nlon))
    wide = in_vmem((EXT_ROWS, 128))
    cx, cy, w0, w1, pw, half, *zeros = call(table_kernel, (grid,) * 5 + (wide,) * (1 + SUMS), [SM] * 4 + [VM] * 2, us=4.0)(
        group_speed, momentum, wind_profile, nonlinear_coef, sea_mask, wind_growth
    )
    quads = [jnp.maximum(quadruplet[r], 0) for r in range(2)]
    sums = in_vmem((16, 128))
    moved, big, small, own = call(
        move_kernel,
        (wide, in_vmem((4 * BORDER, 128)), sums, sums),
        [VM] * 12,
        [pltpu.VMEM((ROWS, 128), F32), pltpu.VMEM((16, 128), F32)],
    )(
        flat, far, near, across, inside, sea_mask, wind_growth, ocean_cell, cx, cy, w0, w1
    )
    their_small = lax.ppermute(small, "freq", swap)
    theirs = lax.ppermute(big, "freq", swap)
    as_bins = lambda x: x.reshape(-1, 4, 128)
    as_rows = lambda x: x.reshape(-1, 128)
    acc = in_vmem((EXT, 4, 128))
    half = as_bins(half)
    parts = call(
        inner_kernel,
        (acc,) * (SUMS + 1),
        [SM] * 2 + [VM] * (2 + SUMS),
        us=3.0,
        aliases={4 + i: i for i in range(SUMS)},
    )(*quads, half, as_bins(moved), *map(as_bins, zeros))

    def gather(rows, bit):
        return lax.ppermute(rows, "lat", [(i, i ^ bit) for i in range(nlat)])

    their_small, *parts = lax.optimization_barrier((their_small, *parts))
    rows = own[0:8] + their_small[0:8]
    other = gather(rows, 1)
    whole = jax.ShapeDtypeStruct((ROWS, 128), F32)
    plain = call(
        plain_kernel,
        whole,
        [VM] * (6 + SUMS),
        [pltpu.VMEM((PLAIN, 128), F32), pltpu.SemaphoreType.DMA((2,))],
        out_specs=ANY,
        us=2.0,
    )(moved, pw, *map(as_rows, parts), own, their_small, dissipation)
    other, plain = lax.optimization_barrier((other, plain))
    rows = jnp.concatenate([rows, other], 0)
    other = gather(rows, 2)
    theirs, rows = lax.optimization_barrier((theirs, rows))
    extended = call(
        extend_kernel,
        (acc,) * (SUMS + 2),
        [SM] * 2 + [VM] * (4 + SUMS),
        us=1.5,
        aliases={4 + i: i for i in range(SUMS + 2)},
    )(*quads, half, as_bins(theirs), as_bins(moved), *parts)
    other, *extended = lax.optimization_barrier((other, *extended))
    rows = jnp.concatenate([rows, other], 0)
    other = gather(rows, 4)
    rows = jnp.concatenate([rows, other], 0)
    out = call(
        outer_kernel,
        whole,
        [VM] * (6 + SUMS) + [ANY],
        [pltpu.VMEM((4 * BORDER, 128), F32), pltpu.SemaphoreType.DMA(())],
        out_specs=ANY,
        us=1.0,
        aliases={6 + SUMS: 0},
    )(as_rows(extended[0]), pw, *map(as_rows, extended[1:]), own, their_small, dissipation, plain)
    stress = call(
        cells_kernel,
        jax.ShapeDtypeStruct((2, 2048), F32),
        [VM],
        [pltpu.VMEM((48, 128), F32), pltpu.VMEM((128, 128), F32)],
    )(rows)
    return out.reshape(spectrum.shape), stress.T


def solution(mesh):
    return jax.shard_map(
        local,
        mesh=mesh,
        in_specs=(
            P("freq", None, "lat", "lon"),
            P("freq"),
            P("lat", "lon"),
            P("lat", "lon"),
            P("lat", "lon"),
            P(),
            P(),
            P(),
            P(),
            P("lat", "lon"),
        ),
        out_specs=(P("freq", None, "lat", "lon"), P(("lon", "freq"), None)),
        check_vma=False,
    )
```

```python
import functools

import jax
import jax.numpy as jnp
import numpy as np
from jax import lax
from jax.experimental import pallas as pl
from jax.experimental.pallas import tpu as pltpu
from jax.sharding import PartitionSpec as P

F32 = jnp.float32
NF, ND = 18, 36
NB = NF * ND
TILES = ND // 2
ROWS = NB * 4
BORDER = 4 * ND

angles = (np.float32(2.0 * np.pi) * np.arange(ND, dtype=np.float32) / np.float32(ND)).astype(np.float32)
COS = np.cos(angles).astype(np.float32)
SIN = np.sin(angles).astype(np.float32)
WEST = [bool(c > 0) for c in COS]
WEST_TILES = [k for k in range(TILES) if WEST[2 * k] or WEST[2 * k + 1]]
EAST_TILES = [k for k in range(TILES) if not (WEST[2 * k] and WEST[2 * k + 1])]
LANES_F = 10
FREQS_V = 6

VM = pl.BlockSpec(memory_space=pltpu.VMEM)
HB = pl.BlockSpec(memory_space=pltpu.HBM)
ANY = pl.BlockSpec(memory_space=pl.ANY)
SM = pl.BlockSpec(memory_space=pltpu.SMEM)
PARAMS = pltpu.CompilerParams(vmem_limit_bytes=16 * 1024 * 1024)


def in_vmem(shape, dtype=F32):
    return pltpu.VMEM(shape, dtype)


def tile_iota(dim):
    return lax.broadcasted_iota(jnp.int32, (8, 128), dim)


def twice(x):
    return jnp.concatenate([x, x], 0)


EXT = 22 * ND
EXT_ROWS = EXT * 4
SUMS = 6
EARLY = 4


def clear(refs, own):
    zero = jnp.zeros((8, 128), F32)

    def one_freq(f, _):
        for k in range(TILES):
            for ref in refs:
                ref[pl.ds(pl.multiple_of(own + f * 144 + k * 8, 8), 8), :] = zero
        return 0

    lax.fori_loop(0, NF, one_freq, 0)


CHUNK = 6


def pack_kernel(hbm_ref, e_ref, raw_ref, far_ref, near_ref, across_ref, inside_ref, *rest):
    *zeros, sems = rest
    lane = tile_iota(1)
    odd_lat = lax.axis_index("lat") % 2 == 1
    odd_lon = lax.axis_index("lon") % 2 == 1
    up, down = 3, 72
    far, near = jnp.where(odd_lat, up, down), jnp.where(odd_lat, down, up)
    copies = []
    for c in range(NF // CHUNK):
        part = pl.ds(c * CHUNK * 144, CHUNK * 144)
        copies.append(pltpu.make_async_copy(hbm_ref.at[part], e_ref.at[part], sems.at[c]))
        copies[c].start()
    clear(zeros, lax.axis_index("freq") * (4 * BORDER))
    acc = [[jnp.zeros((8, 128), F32)] * 3, [jnp.zeros((8, 128), F32)] * 3]
    for f in range(NF):
        if f % CHUNK == 0:
            copies[f // CHUNK].wait()
        far_ref[f * 18 : f * 18 + 18, :] = e_ref[pl.ds(f * 144 + far, 18, stride=4), :]
        near_ref[f * 18 : f * 18 + 18, :] = e_ref[pl.ds(f * 144 + near, 18, stride=4), :]
        chunk = f // FREQS_V
        for side, tiles, col in ((0, WEST_TILES, 127), (1, EAST_TILES, 0)):
            for kk, k in enumerate(tiles):
                pos = (f % FREQS_V) * LANES_F + kk
                x = e_ref[(f * TILES + k) * 8 : (f * TILES + k) * 8 + 8, :]
                acc[side][chunk] = jnp.where(lane == pos, pltpu.roll(x, (pos - col) % 128, 1), acc[side][chunk])
    start = pl.multiple_of((1 - lax.axis_index("freq")) * (14 * 144), 8)
    for k in range(72):
        raw_ref[k * 8 : k * 8 + 8, :] = e_ref[pl.ds(start + k * 8, 8), :]
    for chunk in range(3):
        across_ref[:, chunk * 128 : chunk * 128 + 128] = jnp.where(odd_lon, acc[0][chunk], acc[1][chunk])
        inside_ref[:, chunk * 128 : chunk * 128 + 128] = jnp.where(odd_lon, acc[1][chunk], acc[0][chunk])


def table_kernel(gs_ref, mom_ref, prof_ref, mask_ref, cx_ref, cy_ref, w0_ref, w1_ref, speed_ref):
    freq = lax.axis_index("freq")
    first = freq * NB
    low = tile_iota(0) < 4
    mask8 = twice(mask_ref[...].astype(F32))
    for f in range(4):
        speed_ref[f * 8 : f * 8 + 8, :] = jnp.full((8, 128), gs_ref[(1 - freq) * 14 + f])

    def one_freq(f, _):
        speed = gs_ref[f] * mask8
        for k in range(TILES):
            at = pl.ds(pl.multiple_of(f * 144 + k * 8, 8), 8)
            b = first + f * ND + 2 * k
            cx_ref[at, :] = speed * jnp.where(low, float(abs(COS[2 * k])), float(abs(COS[2 * k + 1])))
            cy_ref[at, :] = speed * jnp.where(low, float(abs(SIN[2 * k])), float(abs(SIN[2 * k + 1])))
            pt = jnp.where(low, prof_ref[b], prof_ref[b + 1])
            w0_ref[at, :] = pt * jnp.where(low, mom_ref[0, b], mom_ref[0, b + 1])
            w1_ref[at, :] = pt * jnp.where(low, mom_ref[1, b], mom_ref[1, b + 1])
        return 0

    lax.fori_loop(0, NF, one_freq, 0)


def input_kernel(prof_ref, wind_ref, _, pw_ref):
    freq = lax.axis_index("freq")
    low = tile_iota(0) < 4
    wind8 = twice(wind_ref[...]) * 0.5

    def one_freq(f, _):
        for k in range(TILES):
            at = pl.ds(pl.multiple_of(f * 144 + k * 8, 8), 8)
            b = freq * NB + f * ND + 2 * k
            pw_ref[at, :] = wind8 * jnp.where(low, prof_ref[b], prof_ref[b + 1])
        return 0

    lax.fori_loop(0, NF, one_freq, 0)


def half_kernel(coef_ref, _, half_ref, *zeros):
    freq = lax.axis_index("freq")
    low = tile_iota(0) < 4

    def one_freq(f, _):
        for k in range(TILES):
            b = freq * (2 * ND) + f * ND + 2 * k
            at = pl.ds(pl.multiple_of(b * 4, 8), 8)
            b = freq * (14 * ND) + b
            half_ref[at, :] = jnp.where(low, 0.5 * coef_ref[b], 0.5 * coef_ref[b + 1])
        return 0

    lax.fori_loop(0, 20, one_freq, 0)
    clear(zeros, freq * (4 * BORDER))


BORDER_HALO = 4 * 18
FIX_ROWS = 2 * BORDER_HALO + 6 * 8


def fix_kernel(far_ref, near_ref, across_ref, inside_ref, speed_ref, fix_ref):
    lower = lax.axis_index("freq") == 0
    for i, ref in enumerate((far_ref, near_ref)):
        fix_ref[i * BORDER_HALO : (i + 1) * BORDER_HALO, :] = jnp.where(
            lower, ref[14 * 18 : 18 * 18, :], ref[0:BORDER_HALO, :]
        )
    for i, ref in enumerate((across_ref, inside_ref)):
        at = 2 * BORDER_HALO + 8 * i
        fix_ref[at : at + 8, :] = jnp.where(lower, pltpu.roll(ref[:, 256:384], 108, 1), ref[:, 0:128])
    at = 2 * BORDER_HALO + 16
    fix_ref[at : at + 32, :] = speed_ref[...]


def neighbours(x, h, hw, he, k, f, places):
    first, last, low, top, bottom = places
    west = east = None
    if k in WEST_TILES:
        pos = f * LANES_F + WEST_TILES.index(k)
        west = jnp.where(first, pltpu.roll(hw, (128 - pos) % 128, 1), pltpu.roll(x, 1, 1))
    if k in EAST_TILES:
        pos = f * LANES_F + EAST_TILES.index(k)
        east = jnp.where(last, pltpu.roll(he, 127 - pos, 1), pltpu.roll(x, 127, 1))
    if east is None:
        side = west
    elif west is None:
        side = east
    else:
        side = jnp.where(low, west, east) if WEST[2 * k] else jnp.where(low, east, west)
    if k < TILES // 2:
        return side, jnp.where(top, h, pltpu.roll(x, 1, 0))
    return side, jnp.where(bottom, h, pltpu.roll(x, 7, 0))


def places_of():
    lane, row = tile_iota(1), tile_iota(0)
    return lane == 0, lane == 127, row < 4, row % 4 == 0, row % 4 == 3


def halo_starts():
    odd = lax.axis_index("lat") % 2 == 1
    south, north = 0, 75
    return jnp.where(odd, north, south), jnp.where(odd, south, north)


def move_kernel(
    e_ref, far_ref, near_ref, across_ref, inside_ref, mask_ref, wind_ref, cell_ref, cx_ref, cy_ref, w0_ref, w1_ref,
    moved_ref, small_ref, own_ref, halo_ref, half_ref,
):
    lat, lon, freq = lax.axis_index("lat"), lax.axis_index("lon"), lax.axis_index("freq")
    lane = tile_iota(1)
    places = places_of()
    odd_lon = lon % 2 == 1
    far, near = halo_starts()
    for f in range(NF):
        halo_ref[pl.ds(f * 144 + far, 18, stride=4), :] = far_ref[f * 18 : f * 18 + 18, :]
        halo_ref[pl.ds(f * 144 + near, 18, stride=4), :] = near_ref[f * 18 : f * 18 + 18, :]
    mask8 = twice(mask_ref[...].astype(F32))
    own = freq * (4 * BORDER)

    def some_freqs(c, carry):
        en, t0, t1 = carry
        across = across_ref[:, pl.ds(pl.multiple_of(c * 128, 128), 128)]
        inside = inside_ref[:, pl.ds(pl.multiple_of(c * 128, 128), 128)]
        hw, he = jnp.where(odd_lon, inside, across), jnp.where(odd_lon, across, inside)
        for f in range(FREQS_V):
            for k in range(TILES):
                at = pl.multiple_of((c * FREQS_V + f) * 144 + k * 8, 8)
                here = pl.ds(at, 8)
                x = e_ref[here, :]
                side, beside = neighbours(x, halo_ref[here, :], hw, he, k, f, places)
                m = mask8 * x - cx_ref[here, :] * (x - side) - cy_ref[here, :] * (x - beside)
                moved_ref[pl.ds(pl.multiple_of(own + at, 8), 8), :] = m
                en = en + m
                t0 = t0 + m * w0_ref[here, :]
                t1 = t1 + m * w1_ref[here, :]
        return en, t0, t1

    zero = jnp.zeros((8, 128), F32)
    en, t0, t1 = lax.fori_loop(0, NF // FREQS_V, some_freqs, (zero, zero, zero))
    wind = wind_ref[...]
    i4 = lax.broadcasted_iota(jnp.int32, (4, 128), 0) + lat * 4
    j4 = lax.broadcasted_iota(jnp.int32, (4, 128), 1) + lon * 128
    offset = cell_ref[...] - (j4 * 32 + i4)
    for c, t in enumerate((t0, t1)):
        tau = (t[0:4] + t[4:8]) * wind
        half_ref[8 * c : 8 * c + 8, :] = zero
        for d in (-1, 0, 1):
            half_ref[8 * c + 1 + d : 8 * c + 5 + d, :] += jnp.where(offset == d, tau, 0.0)
    r0, r1 = half_ref[0:8, :], half_ref[8:16, :]
    lower = jnp.where(lane < 64, r0, pltpu.roll(r1, 64, 1))
    upper = jnp.where(lane < 64, pltpu.roll(r0, 64, 1), r1)
    own_ref[0:8, :] = jnp.where(freq == 0, lower, upper)
    small_ref[0:8, :] = jnp.where(freq == 0, upper, lower)
    total = twice(en[0:4] + en[4:8])
    own_ref[8:16, :] = total
    small_ref[8:16, :] = total


def extend_kernel(raw_ref, fix_ref, mask_ref, _, moved_ref, halo_ref):
    places = places_of()
    low = places[2]
    freq = lax.axis_index("freq")
    far, near = halo_starts()
    for f in range(4):
        halo_ref[pl.ds(f * 144 + far, 18, stride=4), :] = fix_ref[f * 18 : f * 18 + 18, :]
        halo_ref[pl.ds(f * 144 + near, 18, stride=4), :] = fix_ref[BORDER_HALO + f * 18 : BORDER_HALO + f * 18 + 18, :]
    mask8 = twice(mask_ref[...].astype(F32))
    at = 2 * BORDER_HALO
    across, inside = fix_ref[at : at + 8, :], fix_ref[at + 8 : at + 16, :]
    odd_lon = lax.axis_index("lon") % 2 == 1
    hw, he = jnp.where(odd_lon, inside, across), jnp.where(odd_lon, across, inside)
    to = pl.multiple_of((1 - freq) * ROWS, 8)
    for f in range(4):
        speed = fix_ref[at + 16 + f * 8 : at + 24 + f * 8, :] * mask8
        for k in range(TILES):
            here = f * 144 + k * 8
            x = raw_ref[here : here + 8, :]
            side, beside = neighbours(x, halo_ref[here : here + 8, :], hw, he, k, f, places)
            cx = speed * jnp.where(low, float(abs(COS[2 * k])), float(abs(COS[2 * k + 1])))
            cy = speed * jnp.where(low, float(abs(SIN[2 * k])), float(abs(SIN[2 * k + 1])))
            moved_ref[pl.ds(to + here, 8), :] = mask8 * x - cx * (x - side) - cy * (x - beside)


def transfers(own, quads, m_ref, half_ref):
    q0, q1 = quads
    e, third, fourth = [m_ref[b] for b in own], [m_ref[b] for b in q0], [m_ref[b] for b in q1]
    half = [half_ref[b] for b in own]
    return [
        half[i] * (e[i] * (e[i] * (third[i] + fourth[i]) - 2.0 * third[i] * fourth[i])) for i in range(len(own))
    ]


def add_all(quads, t, refs):
    q0, q1 = quads
    n = range(len(t))
    up = [refs[i % 3][q0[i]] for i in n]
    down = [refs[3 + i % 3][q1[i]] for i in n]
    for i in n:
        refs[i % 3][q0[i]] = up[i] + t[i]
    for i in n:
        refs[3 + i % 3][q1[i]] = down[i] + t[i]


SPLIT = 24


def interact_kernel(first, stop, up_ref, down_ref, half_ref, m_ref, *rest):
    refs, t_ref = rest[-SUMS - 1 : -1], rest[-1]
    freq = lax.axis_index("freq")
    start = freq * (2 * ND)
    shift = freq * (14 * ND)

    def one_dir(d, _):
        for group in range(0, 20, 10):
            own = [start + d + f * ND for f in range(group, group + 10)]
            quads = [[ref[shift + b] - shift for b in own] for ref in (up_ref, down_ref)]
            t = transfers(own, quads, m_ref, half_ref)
            add_all(quads, t, refs)
            for b, x in zip(own, t):
                t_ref[b] = x
        return 0

    lax.fori_loop(first, stop, one_dir, 0)


def keep_of(mine_ref, theirs_ref, dis_ref):
    energy = (mine_ref[8:16, :] + theirs_ref[8:16, :]) * (1.0 / (2 * NB))
    return 1.0 - 0.5 * (twice(dis_ref[...]) * energy)


def finish(at, own, keep, m_ref, pw_ref, parts, t_ref):
    here = pl.ds(pl.multiple_of(at, 8), 8)
    total = parts[0][here, :]
    for part in parts[1:]:
        total = total + part[here, :]
    grown = m_ref[here, :] * (keep + pw_ref[pl.ds(pl.multiple_of(at - own, 8), 8), :])
    return grown + (total - 2.0 * t_ref[here, :])


def finish_kernel(m_ref, pw_ref, *rest):
    parts, (t_ref, mine_ref, theirs_ref, dis_ref, hbm_ref, out_ref, sems) = rest[:SUMS], rest[SUMS:]
    own = lax.axis_index("freq") * (4 * BORDER)
    keep = keep_of(mine_ref, theirs_ref, dis_ref)
    copies = []
    for c in range(3):
        def some(f, _):
            for u in range(TILES):
                to = pl.multiple_of((c * FREQS_V + f) * 144 + u * 8, 8)
                out_ref[pl.ds(to, 8), :] = finish(own + to, own, keep, m_ref, pw_ref, parts, t_ref)
            return 0

        lax.fori_loop(0, FREQS_V, some, 0)
        part = pl.ds(c * FREQS_V * 144, FREQS_V * 144)
        copies.append(pltpu.make_async_copy(out_ref.at[part], hbm_ref.at[part], sems.at[c]))
        copies[c].start()
    for copy in copies:
        copy.wait()


def cells_kernel(r_ref, out_ref, z_ref, t_ref):
    lat = lax.axis_index("lat")
    z_ref[...] = jnp.zeros_like(z_ref)
    for k in range(8):
        block = r_ref[pl.ds(pl.multiple_of(jnp.bitwise_xor(lat, k) * 8, 8), 8), :]
        z_ref[7 + 4 * k : 13 + 4 * k, :] += block[0:6]
    t_ref[:, 0:32] = jnp.transpose(z_ref[8:40, :])
    t_ref[:, 32:128] = jnp.zeros((128, 96), F32)
    out = jnp.zeros((32, 128), F32)
    for jj in range(4):
        piece = t_ref[pl.ds(jj, 32, stride=4), :]
        out = out + pltpu.roll(piece, jj * 32, 1)
    for c in range(2):
        for g in range(16):
            out_ref[c : c + 1, g * 128 : g * 128 + 128] = out[c * 16 + g : c * 16 + g + 1, :]


def call(kernel, out, in_specs, scratch=(), out_specs=None, us=1.0, aliases=None):
    return pl.pallas_call(
        kernel,
        out_shape=out,
        in_specs=in_specs,
        out_specs=jax.tree.map(lambda _: VM, out) if out_specs is None else out_specs,
        scratch_shapes=list(scratch),
        compiler_params=PARAMS,
        input_output_aliases=aliases or {},
        cost_estimate=pl.CostEstimate(flops=0, transcendentals=0, bytes_accessed=int(us * 3.0e6)),
    )


def local(
    spectrum, group_speed, sea_mask, wind_growth, dissipation, wind_profile, nonlinear_coef, momentum, quadruplet,
    ocean_cell,
):
    grid = in_vmem((ROWS, 128))
    halo = in_vmem((NF * 18, 128))
    edge = in_vmem((8, 384))
    border = in_vmem((4 * BORDER, 128))
    wide = in_vmem((EXT_ROWS, 128))
    flat, raw, far, near, across, inside, *zeros = call(
        pack_kernel, (grid, border, halo, halo, edge, edge) + (wide,) * EARLY, [HB], [pltpu.SemaphoreType.DMA((NF // CHUNK,))]
    )(pltpu.with_memory_space_constraint(spectrum.reshape(ROWS, 128), pltpu.HBM))
    nlat, nlon = lax.axis_size("lat"), lax.axis_size("lon")

    def pairs(first, count, size):
        both = [(i, (i + 1) % size) for i in range(first, first + 2 * count, 2)]
        return both + [(j, i) for i, j in both]

    swap = pairs(0, 1, 2)
    far = lax.ppermute(far, "lat", pairs(1, nlat // 2 - 1, nlat))
    near = lax.ppermute(near, "lat", pairs(0, nlat // 2, nlat))
    raw = lax.ppermute(raw, "freq", swap)
    across = lax.ppermute(across, "lon", pairs(1, nlon // 2, nlon))
    inside = lax.ppermute(inside, "lon", pairs(0, nlon // 2, nlon))
    sums = in_vmem((16, 128))
    as_bins = lambda x: x.reshape(-1, 4, 128)
    as_rows = lambda x: x.reshape(-1, 128)
    acc = in_vmem((EXT, 4, 128))

    def gather(rows, bit):
        return lax.ppermute(rows, "lat", [(i, i ^ bit) for i in range(nlat)])

    cx, cy, w0, w1, speed = call(table_kernel, (grid,) * 4 + (in_vmem((32, 128)),), [SM] * 3 + [VM], us=2.5)(
        group_speed, momentum, wind_profile, sea_mask
    )
    raw, w1 = lax.optimization_barrier((raw, w1))
    moved, small, own = call(
        move_kernel,
        (wide, sums, sums),
        [VM] * 12,
        [pltpu.VMEM((ROWS, 128), F32), pltpu.VMEM((16, 128), F32)],
        us=1.5,
    )(flat, far, near, across, inside, sea_mask, wind_growth, ocean_cell, cx, cy, w0, w1)
    theirs = lax.ppermute(small, "freq", swap)
    fix = call(fix_kernel, in_vmem((FIX_ROWS, 128)), [VM] * 5, us=0.3)(far, near, across, inside, speed)
    their_fix = lax.ppermute(fix, "freq", swap)
    pw = call(input_kernel, grid, [SM] + [VM] * 2, us=1.5)(wind_profile, wind_growth, fix)
    theirs, pw = lax.optimization_barrier((theirs, pw))
    rows = own[0:8] + theirs[0:8]
    other = gather(rows, 1)
    their_fix, rows = lax.optimization_barrier((their_fix, rows))
    half, *more = call(half_kernel, (wide,) * (1 + SUMS - EARLY), [SM] + [VM], us=1.5)(nonlinear_coef, rows)
    other, half = lax.optimization_barrier((other, half))
    rows = jnp.concatenate([rows, other], 0)
    other = gather(rows, 2)
    their_fix, rows = lax.optimization_barrier((their_fix, rows))
    moved = call(
        extend_kernel, wide, [VM] * 4, [pltpu.VMEM((4 * BORDER, 128), F32)], us=1.0, aliases={3: 0}
    )(raw, their_fix, sea_mask, moved)
    quads = [jnp.maximum(quadruplet[r], 0) for r in range(2)]
    fixed = (*quads, as_bins(half), as_bins(moved))
    parts = list(map(as_bins, (*zeros, *more)))
    for first, stop in ((0, SPLIT), (SPLIT, ND)):
        if first:
            other, *parts = lax.optimization_barrier((other, *parts))
            rows = jnp.concatenate([rows, other], 0)
            other = gather(rows, 4)
            *parts, rows = lax.optimization_barrier((*parts, rows))
        parts = call(
            functools.partial(interact_kernel, first, stop),
            (acc,) * (SUMS + 1),
            [SM] * 2 + [VM] * (2 + len(parts)),
            us=3.0,
            aliases={4 + i: i for i in range(len(parts))},
        )(*fixed, *parts)
    out = call(
        finish_kernel,
        jax.ShapeDtypeStruct((ROWS, 128), F32),
        [VM] * (6 + SUMS),
        [pltpu.VMEM((ROWS, 128), F32), pltpu.SemaphoreType.DMA((3,))],
        out_specs=ANY,
        us=2.0,
    )(moved, pw, *map(as_rows, parts), own, theirs, dissipation)
    other, out = lax.optimization_barrier((other, out))
    stress = call(
        cells_kernel,
        jax.ShapeDtypeStruct((2, 2048), F32),
        [VM],
        [pltpu.VMEM((48, 128), F32), pltpu.VMEM((128, 128), F32)],
    )(jnp.concatenate([rows, other], 0))
    return out.reshape(spectrum.shape), stress.T


def solution(mesh):
    return jax.shard_map(
        local,
        mesh=mesh,
        in_specs=(
            P("freq", None, "lat", "lon"),
            P("freq"),
            P("lat", "lon"),
            P("lat", "lon"),
            P("lat", "lon"),
            P(),
            P(),
            P(),
            P(),
            P("lat", "lon"),
        ),
        out_specs=(P("freq", None, "lat", "lon"), P(("lon", "freq"), None)),
        check_vma=False,
    )
```

```python
import functools

import jax
import jax.numpy as jnp
import numpy as np
from jax import lax
from jax.experimental import pallas as pl
from jax.experimental.pallas import tpu as pltpu
from jax.sharding import PartitionSpec as P

F32 = jnp.float32
NF, ND = 18, 36
NB = NF * ND
TILES = ND // 2
ROWS = NB * 4
BORDER = 4 * ND

angles = (np.float32(2.0 * np.pi) * np.arange(ND, dtype=np.float32) / np.float32(ND)).astype(np.float32)
COS = np.cos(angles).astype(np.float32)
SIN = np.sin(angles).astype(np.float32)
WEST = [bool(c > 0) for c in COS]
WEST_TILES = [k for k in range(TILES) if WEST[2 * k] or WEST[2 * k + 1]]
EAST_TILES = [k for k in range(TILES) if not (WEST[2 * k] and WEST[2 * k + 1])]
LANES_F = 10
FREQS_V = 6

VM = pl.BlockSpec(memory_space=pltpu.VMEM)
HB = pl.BlockSpec(memory_space=pltpu.HBM)
ANY = pl.BlockSpec(memory_space=pl.ANY)
SM = pl.BlockSpec(memory_space=pltpu.SMEM)
PARAMS = pltpu.CompilerParams(vmem_limit_bytes=16 * 1024 * 1024)


def in_vmem(shape, dtype=F32):
    return pltpu.VMEM(shape, dtype)


def tile_iota(dim):
    return lax.broadcasted_iota(jnp.int32, (8, 128), dim)


def twice(x):
    return jnp.concatenate([x, x], 0)


EXT = 22 * ND
EXT_ROWS = EXT * 4
SUMS = 6
EARLY = 4


def clear(refs, own):
    zero = jnp.zeros((8, 128), F32)

    def one_freq(f, _):
        for k in range(TILES):
            for ref in refs:
                ref[pl.ds(pl.multiple_of(own + f * 144 + k * 8, 8), 8), :] = zero
        return 0

    lax.fori_loop(0, NF, one_freq, 0)


CHUNK = 6


SMALL = 8


def pack_kernel(hbm_ref, *rest):
    small_hbm, rest = rest[:SMALL], rest[SMALL:]
    e_ref, raw_ref, far_ref, near_ref, across_ref, inside_ref = rest[:6]
    zeros, small_refs, (sems, small_sems) = rest[6 : 6 + EARLY], rest[6 + EARLY : -2], rest[-2:]
    lane = tile_iota(1)
    odd_lat = lax.axis_index("lat") % 2 == 1
    odd_lon = lax.axis_index("lon") % 2 == 1
    up, down = 3, 72
    far, near = jnp.where(odd_lat, up, down), jnp.where(odd_lat, down, up)
    copies = []
    for c in range(NF // CHUNK):
        part = pl.ds(c * CHUNK * 144, CHUNK * 144)
        copies.append(pltpu.make_async_copy(hbm_ref.at[part], e_ref.at[part], sems.at[c]))
        copies[c].start()
    smalls = [pltpu.make_async_copy(a, b, small_sems.at[i]) for i, (a, b) in enumerate(zip(small_hbm, small_refs))]
    for copy in smalls:
        copy.start()
    clear(zeros, lax.axis_index("freq") * (4 * BORDER))
    acc = [[jnp.zeros((8, 128), F32)] * 3, [jnp.zeros((8, 128), F32)] * 3]
    for f in range(NF):
        if f % CHUNK == 0:
            copies[f // CHUNK].wait()
        far_ref[f * 18 : f * 18 + 18, :] = e_ref[pl.ds(f * 144 + far, 18, stride=4), :]
        near_ref[f * 18 : f * 18 + 18, :] = e_ref[pl.ds(f * 144 + near, 18, stride=4), :]
        chunk = f // FREQS_V
        for side, tiles, col in ((0, WEST_TILES, 127), (1, EAST_TILES, 0)):
            for kk, k in enumerate(tiles):
                pos = (f % FREQS_V) * LANES_F + kk
                x = e_ref[(f * TILES + k) * 8 : (f * TILES + k) * 8 + 8, :]
                acc[side][chunk] = jnp.where(lane == pos, pltpu.roll(x, (pos - col) % 128, 1), acc[side][chunk])
    start = pl.multiple_of((1 - lax.axis_index("freq")) * (14 * 144), 8)
    for k in range(72):
        raw_ref[k * 8 : k * 8 + 8, :] = e_ref[pl.ds(start + k * 8, 8), :]
    for chunk in range(3):
        across_ref[:, chunk * 128 : chunk * 128 + 128] = jnp.where(odd_lon, acc[0][chunk], acc[1][chunk])
        inside_ref[:, chunk * 128 : chunk * 128 + 128] = jnp.where(odd_lon, acc[1][chunk], acc[0][chunk])
    for copy in smalls:
        copy.wait()


def table_kernel(gs_ref, mom_ref, prof_ref, mask_ref, cx_ref, cy_ref, w0_ref, w1_ref, speed_ref):
    freq = lax.axis_index("freq")
    first = freq * NB
    low = tile_iota(0) < 4
    mask8 = twice(mask_ref[...].astype(F32))
    for f in range(4):
        speed_ref[f * 8 : f * 8 + 8, :] = jnp.full((8, 128), gs_ref[(1 - freq) * 14 + f])

    def one_freq(f, _):
        speed = gs_ref[f] * mask8
        for k in range(TILES):
            at = pl.ds(pl.multiple_of(f * 144 + k * 8, 8), 8)
            b = first + f * ND + 2 * k
            cx_ref[at, :] = speed * jnp.where(low, float(abs(COS[2 * k])), float(abs(COS[2 * k + 1])))
            cy_ref[at, :] = speed * jnp.where(low, float(abs(SIN[2 * k])), float(abs(SIN[2 * k + 1])))
            pt = jnp.where(low, prof_ref[b], prof_ref[b + 1])
            w0_ref[at, :] = pt * jnp.where(low, mom_ref[0, b], mom_ref[0, b + 1])
            w1_ref[at, :] = pt * jnp.where(low, mom_ref[1, b], mom_ref[1, b + 1])
        return 0

    lax.fori_loop(0, NF, one_freq, 0)


def input_kernel(prof_ref, wind_ref, _, pw_ref):
    freq = lax.axis_index("freq")
    low = tile_iota(0) < 4
    wind8 = twice(wind_ref[...]) * 0.5

    def one_freq(f, _):
        for k in range(TILES):
            at = pl.ds(pl.multiple_of(f * 144 + k * 8, 8), 8)
            b = freq * NB + f * ND + 2 * k
            pw_ref[at, :] = wind8 * jnp.where(low, prof_ref[b], prof_ref[b + 1])
        return 0

    lax.fori_loop(0, NF, one_freq, 0)


def half_kernel(coef_ref, _, half_ref, *zeros):
    freq = lax.axis_index("freq")
    low = tile_iota(0) < 4

    def one_freq(f, _):
        for k in range(TILES):
            b = freq * (2 * ND) + f * ND + 2 * k
            at = pl.ds(pl.multiple_of(b * 4, 8), 8)
            b = freq * (14 * ND) + b
            half_ref[at, :] = jnp.where(low, 0.5 * coef_ref[b], 0.5 * coef_ref[b + 1])
        return 0

    lax.fori_loop(0, 20, one_freq, 0)
    clear(zeros, freq * (4 * BORDER))


BORDER_HALO = 4 * 18
FIX_ROWS = 2 * BORDER_HALO + 6 * 8


def fix_kernel(far_ref, near_ref, across_ref, inside_ref, speed_ref, fix_ref):
    lower = lax.axis_index("freq") == 0
    for i, ref in enumerate((far_ref, near_ref)):
        fix_ref[i * BORDER_HALO : (i + 1) * BORDER_HALO, :] = jnp.where(
            lower, ref[14 * 18 : 18 * 18, :], ref[0:BORDER_HALO, :]
        )
    for i, ref in enumerate((across_ref, inside_ref)):
        at = 2 * BORDER_HALO + 8 * i
        fix_ref[at : at + 8, :] = jnp.where(lower, pltpu.roll(ref[:, 256:384], 108, 1), ref[:, 0:128])
    at = 2 * BORDER_HALO + 16
    fix_ref[at : at + 32, :] = speed_ref[...]


def neighbours(x, h, hw, he, k, f, places):
    first, last, low, top, bottom = places
    west = east = None
    if k in WEST_TILES:
        pos = f * LANES_F + WEST_TILES.index(k)
        west = jnp.where(first, pltpu.roll(hw, (128 - pos) % 128, 1), pltpu.roll(x, 1, 1))
    if k in EAST_TILES:
        pos = f * LANES_F + EAST_TILES.index(k)
        east = jnp.where(last, pltpu.roll(he, 127 - pos, 1), pltpu.roll(x, 127, 1))
    if east is None:
        side = west
    elif west is None:
        side = east
    else:
        side = jnp.where(low, west, east) if WEST[2 * k] else jnp.where(low, east, west)
    if k < TILES // 2:
        return side, jnp.where(top, h, pltpu.roll(x, 1, 0))
    return side, jnp.where(bottom, h, pltpu.roll(x, 7, 0))


def places_of():
    lane, row = tile_iota(1), tile_iota(0)
    return lane == 0, lane == 127, row < 4, row % 4 == 0, row % 4 == 3


def halo_starts():
    odd = lax.axis_index("lat") % 2 == 1
    south, north = 0, 75
    return jnp.where(odd, north, south), jnp.where(odd, south, north)


def move_kernel(
    e_ref, far_ref, near_ref, across_ref, inside_ref, mask_ref, wind_ref, cell_ref, cx_ref, cy_ref, w0_ref, w1_ref,
    moved_ref, small_ref, own_ref, halo_ref, half_ref,
):
    lat, lon, freq = lax.axis_index("lat"), lax.axis_index("lon"), lax.axis_index("freq")
    lane = tile_iota(1)
    places = places_of()
    odd_lon = lon % 2 == 1
    far, near = halo_starts()
    for f in range(NF):
        halo_ref[pl.ds(f * 144 + far, 18, stride=4), :] = far_ref[f * 18 : f * 18 + 18, :]
        halo_ref[pl.ds(f * 144 + near, 18, stride=4), :] = near_ref[f * 18 : f * 18 + 18, :]
    mask8 = twice(mask_ref[...].astype(F32))
    own = freq * (4 * BORDER)

    def some_freqs(c, carry):
        en, t0, t1 = carry
        across = across_ref[:, pl.ds(pl.multiple_of(c * 128, 128), 128)]
        inside = inside_ref[:, pl.ds(pl.multiple_of(c * 128, 128), 128)]
        hw, he = jnp.where(odd_lon, inside, across), jnp.where(odd_lon, across, inside)
        for f in range(FREQS_V):
            for k in range(TILES):
                at = pl.multiple_of((c * FREQS_V + f) * 144 + k * 8, 8)
                here = pl.ds(at, 8)
                x = e_ref[here, :]
                side, beside = neighbours(x, halo_ref[here, :], hw, he, k, f, places)
                m = mask8 * x - cx_ref[here, :] * (x - side) - cy_ref[here, :] * (x - beside)
                moved_ref[pl.ds(pl.multiple_of(own + at, 8), 8), :] = m
                en = en + m
                t0 = t0 + m * w0_ref[here, :]
                t1 = t1 + m * w1_ref[here, :]
        return en, t0, t1

    zero = jnp.zeros((8, 128), F32)
    en, t0, t1 = lax.fori_loop(0, NF // FREQS_V, some_freqs, (zero, zero, zero))
    wind = wind_ref[...]
    i4 = lax.broadcasted_iota(jnp.int32, (4, 128), 0) + lat * 4
    j4 = lax.broadcasted_iota(jnp.int32, (4, 128), 1) + lon * 128
    offset = cell_ref[...] - (j4 * 32 + i4)
    for c, t in enumerate((t0, t1)):
        tau = (t[0:4] + t[4:8]) * wind
        half_ref[8 * c : 8 * c + 8, :] = zero
        for d in (-1, 0, 1):
            half_ref[8 * c + 1 + d : 8 * c + 5 + d, :] += jnp.where(offset == d, tau, 0.0)
    r0, r1 = half_ref[0:8, :], half_ref[8:16, :]
    lower = jnp.where(lane < 64, r0, pltpu.roll(r1, 64, 1))
    upper = jnp.where(lane < 64, pltpu.roll(r0, 64, 1), r1)
    own_ref[0:8, :] = jnp.where(freq == 0, lower, upper)
    small_ref[0:8, :] = jnp.where(freq == 0, upper, lower)
    total = twice(en[0:4] + en[4:8])
    own_ref[8:16, :] = total
    small_ref[8:16, :] = total


def extend_kernel(raw_ref, fix_ref, mask_ref, _, moved_ref, halo_ref):
    places = places_of()
    low = places[2]
    freq = lax.axis_index("freq")
    far, near = halo_starts()
    for f in range(4):
        halo_ref[pl.ds(f * 144 + far, 18, stride=4), :] = fix_ref[f * 18 : f * 18 + 18, :]
        halo_ref[pl.ds(f * 144 + near, 18, stride=4), :] = fix_ref[BORDER_HALO + f * 18 : BORDER_HALO + f * 18 + 18, :]
    mask8 = twice(mask_ref[...].astype(F32))
    at = 2 * BORDER_HALO
    across, inside = fix_ref[at : at + 8, :], fix_ref[at + 8 : at + 16, :]
    odd_lon = lax.axis_index("lon") % 2 == 1
    hw, he = jnp.where(odd_lon, inside, across), jnp.where(odd_lon, across, inside)
    to = pl.multiple_of((1 - freq) * ROWS, 8)
    for f in range(4):
        speed = fix_ref[at + 16 + f * 8 : at + 24 + f * 8, :] * mask8
        for k in range(TILES):
            here = f * 144 + k * 8
            x = raw_ref[here : here + 8, :]
            side, beside = neighbours(x, halo_ref[here : here + 8, :], hw, he, k, f, places)
            cx = speed * jnp.where(low, float(abs(COS[2 * k])), float(abs(COS[2 * k + 1])))
            cy = speed * jnp.where(low, float(abs(SIN[2 * k])), float(abs(SIN[2 * k + 1])))
            moved_ref[pl.ds(to + here, 8), :] = mask8 * x - cx * (x - side) - cy * (x - beside)


def transfers(own, quads, m_ref, half_ref):
    q0, q1 = quads
    e, third, fourth = [m_ref[b] for b in own], [m_ref[b] for b in q0], [m_ref[b] for b in q1]
    half = [half_ref[b] for b in own]
    return [
        half[i] * (e[i] * (e[i] * (third[i] + fourth[i]) - 2.0 * third[i] * fourth[i])) for i in range(len(own))
    ]


def add_all(quads, t, refs):
    q0, q1 = quads
    n = range(len(t))
    up = [refs[i % 3][q0[i]] for i in n]
    down = [refs[3 + i % 3][q1[i]] for i in n]
    for i in n:
        refs[i % 3][q0[i]] = up[i] + t[i]
    for i in n:
        refs[3 + i % 3][q1[i]] = down[i] + t[i]


SPLIT = 24


def interact_kernel(first, stop, up_ref, down_ref, half_ref, m_ref, *rest):
    refs, t_ref = rest[-SUMS - 1 : -1], rest[-1]
    freq = lax.axis_index("freq")
    start = freq * (2 * ND)
    shift = freq * (14 * ND)

    def one_dir(d, _):
        for group in range(0, 20, 10):
            own = [start + d + f * ND for f in range(group, group + 10)]
            quads = [[ref[shift + b] - shift for b in own] for ref in (up_ref, down_ref)]
            t = transfers(own, quads, m_ref, half_ref)
            add_all(quads, t, refs)
            for b, x in zip(own, t):
                t_ref[b] = x
        return 0

    lax.fori_loop(first, stop, one_dir, 0)


def keep_of(mine_ref, theirs_ref, dis_ref):
    energy = (mine_ref[8:16, :] + theirs_ref[8:16, :]) * (1.0 / (2 * NB))
    return 1.0 - 0.5 * (twice(dis_ref[...]) * energy)


def finish(at, own, keep, m_ref, pw_ref, parts, t_ref):
    here = pl.ds(pl.multiple_of(at, 8), 8)
    total = parts[0][here, :]
    for part in parts[1:]:
        total = total + part[here, :]
    grown = m_ref[here, :] * (keep + pw_ref[pl.ds(pl.multiple_of(at - own, 8), 8), :])
    return grown + (total - 2.0 * t_ref[here, :])


def finish_kernel(m_ref, pw_ref, *rest):
    parts, (t_ref, mine_ref, theirs_ref, dis_ref, hbm_ref, out_ref, sems) = rest[:SUMS], rest[SUMS:]
    own = lax.axis_index("freq") * (4 * BORDER)
    keep = keep_of(mine_ref, theirs_ref, dis_ref)
    copies = []
    for c in range(3):
        def some(f, _):
            for u in range(TILES):
                to = pl.multiple_of((c * FREQS_V + f) * 144 + u * 8, 8)
                out_ref[pl.ds(to, 8), :] = finish(own + to, own, keep, m_ref, pw_ref, parts, t_ref)
            return 0

        lax.fori_loop(0, FREQS_V, some, 0)
        part = pl.ds(c * FREQS_V * 144, FREQS_V * 144)
        copies.append(pltpu.make_async_copy(out_ref.at[part], hbm_ref.at[part], sems.at[c]))
        copies[c].start()
    for copy in copies:
        copy.wait()


def cells_kernel(r_ref, out_ref, z_ref, t_ref):
    lat = lax.axis_index("lat")
    z_ref[...] = jnp.zeros_like(z_ref)
    for k in range(8):
        block = r_ref[pl.ds(pl.multiple_of(jnp.bitwise_xor(lat, k) * 8, 8), 8), :]
        z_ref[7 + 4 * k : 13 + 4 * k, :] += block[0:6]
    t_ref[:, 0:32] = jnp.transpose(z_ref[8:40, :])
    t_ref[:, 32:128] = jnp.zeros((128, 96), F32)
    out = jnp.zeros((32, 128), F32)
    for jj in range(4):
        piece = t_ref[pl.ds(jj, 32, stride=4), :]
        out = out + pltpu.roll(piece, jj * 32, 1)
    for c in range(2):
        for g in range(16):
            out_ref[c : c + 1, g * 128 : g * 128 + 128] = out[c * 16 + g : c * 16 + g + 1, :]


def call(kernel, out, in_specs, scratch=(), out_specs=None, us=1.0, aliases=None):
    return pl.pallas_call(
        kernel,
        out_shape=out,
        in_specs=in_specs,
        out_specs=jax.tree.map(lambda _: VM, out) if out_specs is None else out_specs,
        scratch_shapes=list(scratch),
        compiler_params=PARAMS,
        input_output_aliases=aliases or {},
        cost_estimate=pl.CostEstimate(flops=0, transcendentals=0, bytes_accessed=int(us * 3.0e6)),
    )


def local(
    spectrum, group_speed, sea_mask, wind_growth, dissipation, wind_profile, nonlinear_coef, momentum, quadruplet,
    ocean_cell,
):
    grid = in_vmem((ROWS, 128))
    halo = in_vmem((NF * 18, 128))
    edge = in_vmem((8, 384))
    border = in_vmem((4 * BORDER, 128))
    wide = in_vmem((EXT_ROWS, 128))
    small_args = (
        group_speed, momentum, wind_profile, nonlinear_coef, sea_mask, wind_growth, dissipation, ocean_cell
    )
    flat, raw, far, near, across, inside, *rest = call(
        pack_kernel,
        (grid, border, halo, halo, edge, edge) + (wide,) * EARLY + tuple(in_vmem(x.shape, x.dtype) for x in small_args),
        [HB] * (1 + SMALL),
        [pltpu.SemaphoreType.DMA((NF // CHUNK,)), pltpu.SemaphoreType.DMA((SMALL,))],
    )(*(pltpu.with_memory_space_constraint(x, pltpu.HBM) for x in (spectrum.reshape(ROWS, 128), *small_args)))
    zeros = rest[:EARLY]
    group_speed, momentum, wind_profile, nonlinear_coef, sea_mask, wind_growth, dissipation, ocean_cell = rest[EARLY:]
    nlat, nlon = lax.axis_size("lat"), lax.axis_size("lon")

    def pairs(first, count, size):
        both = [(i, (i + 1) % size) for i in range(first, first + 2 * count, 2)]
        return both + [(j, i) for i, j in both]

    swap = pairs(0, 1, 2)
    far = lax.ppermute(far, "lat", pairs(1, nlat // 2 - 1, nlat))
    near = lax.ppermute(near, "lat", pairs(0, nlat // 2, nlat))
    raw = lax.ppermute(raw, "freq", swap)
    across = lax.ppermute(across, "lon", pairs(1, nlon // 2, nlon))
    inside = lax.ppermute(inside, "lon", pairs(0, nlon // 2, nlon))
    sums = in_vmem((16, 128))
    as_bins = lambda x: x.reshape(-1, 4, 128)
    as_rows = lambda x: x.reshape(-1, 128)
    acc = in_vmem((EXT, 4, 128))

    def gather(rows, bit):
        return lax.ppermute(rows, "lat", [(i, i ^ bit) for i in range(nlat)])

    cx, cy, w0, w1, speed = call(table_kernel, (grid,) * 4 + (in_vmem((32, 128)),), [SM] * 3 + [VM], us=2.5)(
        group_speed, momentum, wind_profile, sea_mask
    )
    raw, w1 = lax.optimization_barrier((raw, w1))
    moved, small, own = call(
        move_kernel,
        (wide, sums, sums),
        [VM] * 12,
        [pltpu.VMEM((ROWS, 128), F32), pltpu.VMEM((16, 128), F32)],
        us=1.5,
    )(flat, far, near, across, inside, sea_mask, wind_growth, ocean_cell, cx, cy, w0, w1)
    theirs = lax.ppermute(small, "freq", swap)
    fix = call(fix_kernel, in_vmem((FIX_ROWS, 128)), [VM] * 5, us=0.3)(far, near, across, inside, speed)
    their_fix = lax.ppermute(fix, "freq", swap)
    pw = call(input_kernel, grid, [SM] + [VM] * 2, us=1.5)(wind_profile, wind_growth, fix)
    theirs, pw = lax.optimization_barrier((theirs, pw))
    rows = own[0:8] + theirs[0:8]
    other = gather(rows, 1)
    their_fix, rows = lax.optimization_barrier((their_fix, rows))
    half, *more = call(half_kernel, (wide,) * (1 + SUMS - EARLY), [SM] + [VM], us=1.5)(nonlinear_coef, rows)
    other, half = lax.optimization_barrier((other, half))
    rows = jnp.concatenate([rows, other], 0)
    other = gather(rows, 2)
    their_fix, rows = lax.optimization_barrier((their_fix, rows))
    moved = call(
        extend_kernel, wide, [VM] * 4, [pltpu.VMEM((4 * BORDER, 128), F32)], us=1.0, aliases={3: 0}
    )(raw, their_fix, sea_mask, moved)
    quads = [jnp.maximum(quadruplet[r], 0) for r in range(2)]
    fixed = (*quads, as_bins(half), as_bins(moved))
    parts = list(map(as_bins, (*zeros, *more)))
    for first, stop in ((0, SPLIT), (SPLIT, ND)):
        if first:
            other, *parts = lax.optimization_barrier((other, *parts))
            rows = jnp.concatenate([rows, other], 0)
            other = gather(rows, 4)
            *parts, rows = lax.optimization_barrier((*parts, rows))
        parts = call(
            functools.partial(interact_kernel, first, stop),
            (acc,) * (SUMS + 1),
            [SM] * 2 + [VM] * (2 + len(parts)),
            us=3.0,
            aliases={4 + i: i for i in range(len(parts))},
        )(*fixed, *parts)
    out = call(
        finish_kernel,
        jax.ShapeDtypeStruct((ROWS, 128), F32),
        [VM] * (6 + SUMS),
        [pltpu.VMEM((ROWS, 128), F32), pltpu.SemaphoreType.DMA((3,))],
        out_specs=ANY,
        us=2.0,
    )(moved, pw, *map(as_rows, parts), own, theirs, dissipation)
    other, out = lax.optimization_barrier((other, out))
    stress = call(
        cells_kernel,
        jax.ShapeDtypeStruct((2, 2048), F32),
        [VM],
        [pltpu.VMEM((48, 128), F32), pltpu.VMEM((128, 128), F32)],
    )(jnp.concatenate([rows, other], 0))
    return out.reshape(spectrum.shape), stress.T


def solution(mesh):
    return jax.shard_map(
        local,
        mesh=mesh,
        in_specs=(
            P("freq", None, "lat", "lon"),
            P("freq"),
            P("lat", "lon"),
            P("lat", "lon"),
            P("lat", "lon"),
            P(),
            P(),
            P(),
            P(),
            P("lat", "lon"),
        ),
        out_specs=(P("freq", None, "lat", "lon"), P(("lon", "freq"), None)),
        check_vma=False,
    )
```

```python
import functools

import jax
import jax.numpy as jnp
import numpy as np
from jax import lax
from jax.experimental import pallas as pl
from jax.experimental.pallas import tpu as pltpu
from jax.sharding import PartitionSpec as P

F32 = jnp.float32
NF, ND = 18, 36
NB = NF * ND
TILES = ND // 2
ROWS = NB * 4
BORDER = 4 * ND

angles = (np.float32(2.0 * np.pi) * np.arange(ND, dtype=np.float32) / np.float32(ND)).astype(np.float32)
COS = np.cos(angles).astype(np.float32)
SIN = np.sin(angles).astype(np.float32)
WEST = [bool(c > 0) for c in COS]
WEST_TILES = [k for k in range(TILES) if WEST[2 * k] or WEST[2 * k + 1]]
EAST_TILES = [k for k in range(TILES) if not (WEST[2 * k] and WEST[2 * k + 1])]
LANES_F = 10
FREQS_V = 6

VM = pl.BlockSpec(memory_space=pltpu.VMEM)
HB = pl.BlockSpec(memory_space=pltpu.HBM)
ANY = pl.BlockSpec(memory_space=pl.ANY)
SM = pl.BlockSpec(memory_space=pltpu.SMEM)
PARAMS = pltpu.CompilerParams(vmem_limit_bytes=16 * 1024 * 1024)


def in_vmem(shape, dtype=F32):
    return pltpu.VMEM(shape, dtype)


def tile_iota(dim):
    return lax.broadcasted_iota(jnp.int32, (8, 128), dim)


def twice(x):
    return jnp.concatenate([x, x], 0)


EXT = 22 * ND
EXT_ROWS = EXT * 4
SUMS = 6
EARLY = 4


def clear(refs, own):
    zero = jnp.zeros((8, 128), F32)

    def one_freq(f, _):
        for k in range(TILES):
            for ref in refs:
                ref[pl.ds(pl.multiple_of(own + f * 144 + k * 8, 8), 8), :] = zero
        return 0

    lax.fori_loop(0, NF, one_freq, 0)


CHUNK = 6


SMALL = 8


def pack_kernel(hbm_ref, *rest):
    small_hbm, rest = rest[:SMALL], rest[SMALL:]
    e_ref, raw_ref, far_ref, near_ref, across_ref, inside_ref = rest[:6]
    zeros, small_refs, (sems, small_sems) = rest[6 : 6 + EARLY], rest[6 + EARLY : -2], rest[-2:]
    lane = tile_iota(1)
    odd_lat = lax.axis_index("lat") % 2 == 1
    odd_lon = lax.axis_index("lon") % 2 == 1
    up, down = 3, 72
    far, near = jnp.where(odd_lat, up, down), jnp.where(odd_lat, down, up)
    copies = []
    for c in range(NF // CHUNK):
        part = pl.ds(c * CHUNK * 144, CHUNK * 144)
        copies.append(pltpu.make_async_copy(hbm_ref.at[part], e_ref.at[part], sems.at[c]))
        copies[c].start()
    smalls = [pltpu.make_async_copy(a, b, small_sems.at[i]) for i, (a, b) in enumerate(zip(small_hbm, small_refs))]
    for copy in smalls:
        copy.start()
    clear(zeros, lax.axis_index("freq") * (4 * BORDER))
    acc = [[jnp.zeros((8, 128), F32)] * 3, [jnp.zeros((8, 128), F32)] * 3]
    for f in range(NF):
        if f % CHUNK == 0:
            copies[f // CHUNK].wait()
        far_ref[f * 18 : f * 18 + 18, :] = e_ref[pl.ds(f * 144 + far, 18, stride=4), :]
        near_ref[f * 18 : f * 18 + 18, :] = e_ref[pl.ds(f * 144 + near, 18, stride=4), :]
        chunk = f // FREQS_V
        for side, tiles, col in ((0, WEST_TILES, 127), (1, EAST_TILES, 0)):
            for kk, k in enumerate(tiles):
                pos = (f % FREQS_V) * LANES_F + kk
                x = e_ref[(f * TILES + k) * 8 : (f * TILES + k) * 8 + 8, :]
                acc[side][chunk] = jnp.where(lane == pos, pltpu.roll(x, (pos - col) % 128, 1), acc[side][chunk])
    start = pl.multiple_of((1 - lax.axis_index("freq")) * (14 * 144), 8)
    for k in range(72):
        raw_ref[k * 8 : k * 8 + 8, :] = e_ref[pl.ds(start + k * 8, 8), :]
    for chunk in range(3):
        across_ref[:, chunk * 128 : chunk * 128 + 128] = jnp.where(odd_lon, acc[0][chunk], acc[1][chunk])
        inside_ref[:, chunk * 128 : chunk * 128 + 128] = jnp.where(odd_lon, acc[1][chunk], acc[0][chunk])
    for copy in smalls:
        copy.wait()


def table_kernel(gs_ref, mom_ref, prof_ref, mask_ref, cx_ref, cy_ref, w0_ref, w1_ref, speed_ref):
    freq = lax.axis_index("freq")
    first = freq * NB
    low = tile_iota(0) < 4
    mask8 = twice(mask_ref[...].astype(F32))
    for f in range(4):
        speed_ref[f * 2 : f * 2 + 2, :] = jnp.full((2, 128), gs_ref[(1 - freq) * 14 + f])

    def one_freq(f, _):
        speed = gs_ref[f] * mask8
        for k in range(TILES):
            at = pl.ds(pl.multiple_of(f * 144 + k * 8, 8), 8)
            b = first + f * ND + 2 * k
            cx_ref[at, :] = speed * jnp.where(low, float(abs(COS[2 * k])), float(abs(COS[2 * k + 1])))
            cy_ref[at, :] = speed * jnp.where(low, float(abs(SIN[2 * k])), float(abs(SIN[2 * k + 1])))
            pt = jnp.where(low, prof_ref[b], prof_ref[b + 1])
            w0_ref[at, :] = pt * jnp.where(low, mom_ref[0, b], mom_ref[0, b + 1])
            w1_ref[at, :] = pt * jnp.where(low, mom_ref[1, b], mom_ref[1, b + 1])
        return 0

    lax.fori_loop(0, NF, one_freq, 0)


def input_kernel(prof_ref, wind_ref, _, pw_ref):
    freq = lax.axis_index("freq")
    low = tile_iota(0) < 4
    wind8 = twice(wind_ref[...]) * 0.5

    def one_freq(f, _):
        for k in range(TILES):
            at = pl.ds(pl.multiple_of(f * 144 + k * 8, 8), 8)
            b = freq * NB + f * ND + 2 * k
            pw_ref[at, :] = wind8 * jnp.where(low, prof_ref[b], prof_ref[b + 1])
        return 0

    lax.fori_loop(0, NF, one_freq, 0)


def half_kernel(coef_ref, _, half_ref, *zeros):
    freq = lax.axis_index("freq")
    low = tile_iota(0) < 4

    def one_freq(f, _):
        for k in range(TILES):
            b = freq * (2 * ND) + f * ND + 2 * k
            at = pl.ds(pl.multiple_of(b * 4, 8), 8)
            b = freq * (14 * ND) + b
            half_ref[at, :] = jnp.where(low, 0.5 * coef_ref[b], 0.5 * coef_ref[b + 1])
        return 0

    lax.fori_loop(0, 20, one_freq, 0)
    clear(zeros, freq * (4 * BORDER))


BORDER_HALO = 4 * 18
FIX_ROWS = 2 * BORDER_HALO + 3 * 8


def fix_kernel(far_ref, near_ref, across_ref, inside_ref, speed_ref, fix_ref):
    lower = lax.axis_index("freq") == 0
    for i, ref in enumerate((far_ref, near_ref)):
        fix_ref[i * BORDER_HALO : (i + 1) * BORDER_HALO, :] = jnp.where(
            lower, ref[14 * 18 : 18 * 18, :], ref[0:BORDER_HALO, :]
        )
    for i, ref in enumerate((across_ref, inside_ref)):
        at = 2 * BORDER_HALO + 8 * i
        fix_ref[at : at + 8, :] = jnp.where(lower, pltpu.roll(ref[:, 256:384], 108, 1), ref[:, 0:128])
    at = 2 * BORDER_HALO + 16
    fix_ref[at : at + 8, :] = speed_ref[...]


def neighbours(x, h, hw, he, k, f, places):
    first, last, low, top, bottom = places
    west = east = None
    if k in WEST_TILES:
        pos = f * LANES_F + WEST_TILES.index(k)
        west = jnp.where(first, pltpu.roll(hw, (128 - pos) % 128, 1), pltpu.roll(x, 1, 1))
    if k in EAST_TILES:
        pos = f * LANES_F + EAST_TILES.index(k)
        east = jnp.where(last, pltpu.roll(he, 127 - pos, 1), pltpu.roll(x, 127, 1))
    if east is None:
        side = west
    elif west is None:
        side = east
    else:
        side = jnp.where(low, west, east) if WEST[2 * k] else jnp.where(low, east, west)
    if k < TILES // 2:
        return side, jnp.where(top, h, pltpu.roll(x, 1, 0))
    return side, jnp.where(bottom, h, pltpu.roll(x, 7, 0))


def places_of():
    lane, row = tile_iota(1), tile_iota(0)
    return lane == 0, lane == 127, row < 4, row % 4 == 0, row % 4 == 3


def halo_starts():
    odd = lax.axis_index("lat") % 2 == 1
    south, north = 0, 75
    return jnp.where(odd, north, south), jnp.where(odd, south, north)


def move_kernel(
    e_ref, far_ref, near_ref, across_ref, inside_ref, mask_ref, wind_ref, cell_ref, cx_ref, cy_ref, w0_ref, w1_ref,
    moved_ref, small_ref, own_ref, halo_ref, half_ref,
):
    lat, lon, freq = lax.axis_index("lat"), lax.axis_index("lon"), lax.axis_index("freq")
    lane = tile_iota(1)
    places = places_of()
    odd_lon = lon % 2 == 1
    far, near = halo_starts()
    for f in range(NF):
        halo_ref[pl.ds(f * 144 + far, 18, stride=4), :] = far_ref[f * 18 : f * 18 + 18, :]
        halo_ref[pl.ds(f * 144 + near, 18, stride=4), :] = near_ref[f * 18 : f * 18 + 18, :]
    mask8 = twice(mask_ref[...].astype(F32))
    own = freq * (4 * BORDER)

    def some_freqs(c, carry):
        en, t0, t1 = carry
        across = across_ref[:, pl.ds(pl.multiple_of(c * 128, 128), 128)]
        inside = inside_ref[:, pl.ds(pl.multiple_of(c * 128, 128), 128)]
        hw, he = jnp.where(odd_lon, inside, across), jnp.where(odd_lon, across, inside)
        for f in range(FREQS_V):
            for k in range(TILES):
                at = pl.multiple_of((c * FREQS_V + f) * 144 + k * 8, 8)
                here = pl.ds(at, 8)
                x = e_ref[here, :]
                side, beside = neighbours(x, halo_ref[here, :], hw, he, k, f, places)
                m = mask8 * x - cx_ref[here, :] * (x - side) - cy_ref[here, :] * (x - beside)
                moved_ref[pl.ds(pl.multiple_of(own + at, 8), 8), :] = m
                en = en + m
                t0 = t0 + m * w0_ref[here, :]
                t1 = t1 + m * w1_ref[here, :]
        return en, t0, t1

    zero = jnp.zeros((8, 128), F32)
    en, t0, t1 = lax.fori_loop(0, NF // FREQS_V, some_freqs, (zero, zero, zero))
    wind = wind_ref[...]
    i4 = lax.broadcasted_iota(jnp.int32, (4, 128), 0) + lat * 4
    j4 = lax.broadcasted_iota(jnp.int32, (4, 128), 1) + lon * 128
    offset = cell_ref[...] - (j4 * 32 + i4)
    for c, t in enumerate((t0, t1)):
        tau = (t[0:4] + t[4:8]) * wind
        half_ref[8 * c : 8 * c + 8, :] = zero
        for d in (-1, 0, 1):
            half_ref[8 * c + 1 + d : 8 * c + 5 + d, :] += jnp.where(offset == d, tau, 0.0)
    r0, r1 = half_ref[0:8, :], half_ref[8:16, :]
    lower = jnp.where(lane < 64, r0, pltpu.roll(r1, 64, 1))
    upper = jnp.where(lane < 64, pltpu.roll(r0, 64, 1), r1)
    own_ref[0:8, :] = jnp.where(freq == 0, lower, upper)
    small_ref[0:8, :] = jnp.where(freq == 0, upper, lower)
    total = twice(en[0:4] + en[4:8])
    own_ref[8:16, :] = total
    small_ref[8:16, :] = total


def extend_kernel(raw_ref, fix_ref, mask_ref, _, moved_ref, halo_ref):
    places = places_of()
    low = places[2]
    freq = lax.axis_index("freq")
    far, near = halo_starts()
    for f in range(4):
        halo_ref[pl.ds(f * 144 + far, 18, stride=4), :] = fix_ref[f * 18 : f * 18 + 18, :]
        halo_ref[pl.ds(f * 144 + near, 18, stride=4), :] = fix_ref[BORDER_HALO + f * 18 : BORDER_HALO + f * 18 + 18, :]
    mask8 = twice(mask_ref[...].astype(F32))
    at = 2 * BORDER_HALO
    across, inside = fix_ref[at : at + 8, :], fix_ref[at + 8 : at + 16, :]
    odd_lon = lax.axis_index("lon") % 2 == 1
    hw, he = jnp.where(odd_lon, inside, across), jnp.where(odd_lon, across, inside)
    to = pl.multiple_of((1 - freq) * ROWS, 8)
    for f in range(4):
        speed = jnp.broadcast_to(fix_ref[at + 16 + f * 2 : at + 17 + f * 2, :], (8, 128)) * mask8
        for k in range(TILES):
            here = f * 144 + k * 8
            x = raw_ref[here : here + 8, :]
            side, beside = neighbours(x, halo_ref[here : here + 8, :], hw, he, k, f, places)
            cx = speed * jnp.where(low, float(abs(COS[2 * k])), float(abs(COS[2 * k + 1])))
            cy = speed * jnp.where(low, float(abs(SIN[2 * k])), float(abs(SIN[2 * k + 1])))
            moved_ref[pl.ds(to + here, 8), :] = mask8 * x - cx * (x - side) - cy * (x - beside)


def transfers(own, quads, m_ref, half_ref):
    q0, q1 = quads
    e, third, fourth = [m_ref[b] for b in own], [m_ref[b] for b in q0], [m_ref[b] for b in q1]
    half = [half_ref[b] for b in own]
    return [
        half[i] * (e[i] * (e[i] * (third[i] + fourth[i]) - 2.0 * third[i] * fourth[i])) for i in range(len(own))
    ]


def add_all(quads, t, refs):
    q0, q1 = quads
    n = range(len(t))
    up = [refs[i % 3][q0[i]] for i in n]
    down = [refs[3 + i % 3][q1[i]] for i in n]
    for i in n:
        refs[i % 3][q0[i]] = up[i] + t[i]
    for i in n:
        refs[3 + i % 3][q1[i]] = down[i] + t[i]


SPLIT = 24


def interact_kernel(first, stop, up_ref, down_ref, half_ref, m_ref, *rest):
    refs, t_ref = rest[-SUMS - 1 : -1], rest[-1]
    freq = lax.axis_index("freq")
    start = freq * (2 * ND)
    shift = freq * (14 * ND)

    def one_dir(d, _):
        for group in range(0, 20, 10):
            own = [start + d + f * ND for f in range(group, group + 10)]
            quads = [[ref[shift + b] - shift for b in own] for ref in (up_ref, down_ref)]
            t = transfers(own, quads, m_ref, half_ref)
            add_all(quads, t, refs)
            for b, x in zip(own, t):
                t_ref[b] = x
        return 0

    lax.fori_loop(first, stop, one_dir, 0)


def keep_of(mine_ref, theirs_ref, dis_ref):
    energy = (mine_ref[8:16, :] + theirs_ref[8:16, :]) * (1.0 / (2 * NB))
    return 1.0 - 0.5 * (twice(dis_ref[...]) * energy)


def finish(at, own, keep, m_ref, pw_ref, parts, t_ref):
    here = pl.ds(pl.multiple_of(at, 8), 8)
    total = parts[0][here, :]
    for part in parts[1:]:
        total = total + part[here, :]
    grown = m_ref[here, :] * (keep + pw_ref[pl.ds(pl.multiple_of(at - own, 8), 8), :])
    return grown + (total - 2.0 * t_ref[here, :])


def finish_kernel(m_ref, pw_ref, *rest):
    parts, (t_ref, mine_ref, theirs_ref, dis_ref, hbm_ref, out_ref, sems) = rest[:SUMS], rest[SUMS:]
    own = lax.axis_index("freq") * (4 * BORDER)
    keep = keep_of(mine_ref, theirs_ref, dis_ref)
    copies = []
    for c in range(3):
        def some(f, _):
            for u in range(TILES):
                to = pl.multiple_of((c * FREQS_V + f) * 144 + u * 8, 8)
                out_ref[pl.ds(to, 8), :] = finish(own + to, own, keep, m_ref, pw_ref, parts, t_ref)
            return 0

        lax.fori_loop(0, FREQS_V, some, 0)
        part = pl.ds(c * FREQS_V * 144, FREQS_V * 144)
        copies.append(pltpu.make_async_copy(out_ref.at[part], hbm_ref.at[part], sems.at[c]))
        copies[c].start()
    for copy in copies:
        copy.wait()


def cells_kernel(r_ref, out_ref, z_ref, t_ref):
    lat = lax.axis_index("lat")
    z_ref[...] = jnp.zeros_like(z_ref)
    for k in range(8):
        block = r_ref[pl.ds(pl.multiple_of(jnp.bitwise_xor(lat, k) * 8, 8), 8), :]
        z_ref[7 + 4 * k : 13 + 4 * k, :] += block[0:6]
    t_ref[:, 0:32] = jnp.transpose(z_ref[8:40, :])
    t_ref[:, 32:128] = jnp.zeros((128, 96), F32)
    out = jnp.zeros((32, 128), F32)
    for jj in range(4):
        piece = t_ref[pl.ds(jj, 32, stride=4), :]
        out = out + pltpu.roll(piece, jj * 32, 1)
    for c in range(2):
        for g in range(16):
            out_ref[c : c + 1, g * 128 : g * 128 + 128] = out[c * 16 + g : c * 16 + g + 1, :]


def call(kernel, out, in_specs, scratch=(), out_specs=None, us=1.0, aliases=None):
    return pl.pallas_call(
        kernel,
        out_shape=out,
        in_specs=in_specs,
        out_specs=jax.tree.map(lambda _: VM, out) if out_specs is None else out_specs,
        scratch_shapes=list(scratch),
        compiler_params=PARAMS,
        input_output_aliases=aliases or {},
        cost_estimate=pl.CostEstimate(flops=0, transcendentals=0, bytes_accessed=int(us * 3.0e6)),
    )


def local(
    spectrum, group_speed, sea_mask, wind_growth, dissipation, wind_profile, nonlinear_coef, momentum, quadruplet,
    ocean_cell,
):
    grid = in_vmem((ROWS, 128))
    halo = in_vmem((NF * 18, 128))
    edge = in_vmem((8, 384))
    border = in_vmem((4 * BORDER, 128))
    wide = in_vmem((EXT_ROWS, 128))
    small_args = (
        group_speed, momentum, wind_profile, nonlinear_coef, sea_mask, wind_growth, dissipation, ocean_cell
    )
    flat, raw, far, near, across, inside, *rest = call(
        pack_kernel,
        (grid, border, halo, halo, edge, edge) + (wide,) * EARLY + tuple(in_vmem(x.shape, x.dtype) for x in small_args),
        [HB] * (1 + SMALL),
        [pltpu.SemaphoreType.DMA((NF // CHUNK,)), pltpu.SemaphoreType.DMA((SMALL,))],
    )(*(pltpu.with_memory_space_constraint(x, pltpu.HBM) for x in (spectrum.reshape(ROWS, 128), *small_args)))
    zeros = rest[:EARLY]
    group_speed, momentum, wind_profile, nonlinear_coef, sea_mask, wind_growth, dissipation, ocean_cell = rest[EARLY:]
    nlat, nlon = lax.axis_size("lat"), lax.axis_size("lon")

    def pairs(first, count, size):
        both = [(i, (i + 1) % size) for i in range(first, first + 2 * count, 2)]
        return both + [(j, i) for i, j in both]

    swap = pairs(0, 1, 2)
    far = lax.ppermute(far, "lat", pairs(1, nlat // 2 - 1, nlat))
    near = lax.ppermute(near, "lat", pairs(0, nlat // 2, nlat))
    raw = lax.ppermute(raw, "freq", swap)
    across = lax.ppermute(across, "lon", pairs(1, nlon // 2, nlon))
    inside = lax.ppermute(inside, "lon", pairs(0, nlon // 2, nlon))
    sums = in_vmem((16, 128))
    as_bins = lambda x: x.reshape(-1, 4, 128)
    as_rows = lambda x: x.reshape(-1, 128)
    acc = in_vmem((EXT, 4, 128))

    def gather(rows, bit):
        return lax.ppermute(rows, "lat", [(i, i ^ bit) for i in range(nlat)])

    cx, cy, w0, w1, speed = call(table_kernel, (grid,) * 4 + (in_vmem((8, 128)),), [SM] * 3 + [VM], us=2.5)(
        group_speed, momentum, wind_profile, sea_mask
    )
    raw, w1 = lax.optimization_barrier((raw, w1))
    moved, small, own = call(
        move_kernel,
        (wide, sums, sums),
        [VM] * 12,
        [pltpu.VMEM((ROWS, 128), F32), pltpu.VMEM((16, 128), F32)],
        us=1.5,
    )(flat, far, near, across, inside, sea_mask, wind_growth, ocean_cell, cx, cy, w0, w1)
    theirs = lax.ppermute(small, "freq", swap)
    fix = call(fix_kernel, in_vmem((FIX_ROWS, 128)), [VM] * 5, us=0.3)(far, near, across, inside, speed)
    their_fix = lax.ppermute(fix, "freq", swap)
    pw = call(input_kernel, grid, [SM] + [VM] * 2, us=1.5)(wind_profile, wind_growth, fix)
    theirs, pw = lax.optimization_barrier((theirs, pw))
    rows = own[0:8] + theirs[0:8]
    other = gather(rows, 1)
    their_fix, rows = lax.optimization_barrier((their_fix, rows))
    half, *more = call(half_kernel, (wide,) * (1 + SUMS - EARLY), [SM] + [VM], us=1.5)(nonlinear_coef, rows)
    other, half = lax.optimization_barrier((other, half))
    rows = jnp.concatenate([rows, other], 0)
    other = gather(rows, 2)
    their_fix, rows = lax.optimization_barrier((their_fix, rows))
    moved = call(
        extend_kernel, wide, [VM] * 4, [pltpu.VMEM((4 * BORDER, 128), F32)], us=1.0, aliases={3: 0}
    )(raw, their_fix, sea_mask, moved)
    quads = [jnp.maximum(quadruplet[r], 0) for r in range(2)]
    fixed = (*quads, as_bins(half), as_bins(moved))
    parts = list(map(as_bins, (*zeros, *more)))
    for first, stop in ((0, SPLIT), (SPLIT, ND)):
        if first:
            other, *parts = lax.optimization_barrier((other, *parts))
            rows = jnp.concatenate([rows, other], 0)
            other = gather(rows, 4)
            *parts, rows = lax.optimization_barrier((*parts, rows))
        parts = call(
            functools.partial(interact_kernel, first, stop),
            (acc,) * (SUMS + 1),
            [SM] * 2 + [VM] * (2 + len(parts)),
            us=3.0,
            aliases={4 + i: i for i in range(len(parts))},
        )(*fixed, *parts)
    out = call(
        finish_kernel,
        jax.ShapeDtypeStruct((ROWS, 128), F32),
        [VM] * (6 + SUMS),
        [pltpu.VMEM((ROWS, 128), F32), pltpu.SemaphoreType.DMA((3,))],
        out_specs=ANY,
        us=2.0,
    )(moved, pw, *map(as_rows, parts), own, theirs, dissipation)
    other, out = lax.optimization_barrier((other, out))
    stress = call(
        cells_kernel,
        jax.ShapeDtypeStruct((2, 2048), F32),
        [VM],
        [pltpu.VMEM((48, 128), F32), pltpu.VMEM((128, 128), F32)],
    )(jnp.concatenate([rows, other], 0))
    return out.reshape(spectrum.shape), stress.T


def solution(mesh):
    return jax.shard_map(
        local,
        mesh=mesh,
        in_specs=(
            P("freq", None, "lat", "lon"),
            P("freq"),
            P("lat", "lon"),
            P("lat", "lon"),
            P("lat", "lon"),
            P(),
            P(),
            P(),
            P(),
            P("lat", "lon"),
        ),
        out_specs=(P("freq", None, "lat", "lon"), P(("lon", "freq"), None)),
        check_vma=False,
    )
```
